256 devices in a mesh: cable: 32 (over y_lo, z, core), grid: 8 (over x, y_hi).
Axes of the slice: x: 4, y: 4 (y_hi: 2, y_lo: 2; y = y_hi * 2 + y_lo), z: 8, core: 2. Of those that a mesh axis runs over, the one named last changes fastest.
Arguments:
- green: bfloat16 [2, 8192, 16384], P(None, 'cable', 'grid'), may hold values from -6 to 6
- source_weight: float32 [16384], P('grid'), may hold values from 0.25 to 4
- observed: float32 [2, 2, 8192, 256], P(None, None, 'cable'), may hold values from -6 to 6
- amp_weight: float32 [2, 8192, 256], P(None, 'cable'), may hold values from 0.25 to 2
- pair_used: int32 [32, 2], P('cable'), may hold values 0 or 1
Outputs:
- adjoint: float32 [2, 8192, 16384], P(None, 'cable', 'grid')
- kernel: float32 [16384], P('grid')
The draws below stay inside these ranges and needn't reach their ends.
All inputs are finite; a program needn't handle non-finite values. No bound on the sum of `pair_used` on one device may be relied on, other than what follows from the above.
Results may differ from the reference program's by a relative error of at most 0.0037.
Values may be sent and summed in bfloat16 or wider, within the bound.
No kernel may reach another device: no remote copies, remote signals or barrier semaphores. Data moves between devices by JAX's collectives and lax.ppermute only.
A program may use at most 64 MiB of HBM per device.

```python
import math
import jax
import jax.numpy as jnp
from jax import lax

NR = 256
NB = 32
RECV = 8192
GRID = 16384
N_CABLE = 32


def place_ends(drawn, own_key, smallest, top_value):
    longest = drawn.shape.index(max(drawn.shape))
    spots = []
    for shift in (0, 1):
        where = [jax.random.randint(jax.random.fold_in(own_key, axis), (), 0, length) for axis, length in enumerate(drawn.shape)]
        where[longest] = (where[longest] + shift) % drawn.shape[longest]
        spots.append(tuple(where))
    return drawn.at[spots[0]].set(smallest).at[spots[1]].set(top_value)


def levels(key, shape, split, low, largest):
    def one(position, parts):
        heights = jax.random.uniform(jax.random.fold_in(jax.random.fold_in(key, 6), position), (parts,), jnp.float32, low / len(split), largest / len(split))
        return jnp.repeat(jnp.exp(heights), shape[position] // parts).reshape((-1,) + (1,) * (len(shape) - position - 1))

    level = one(*split[0])
    for cut in split[1:]:
        level = level * one(*cut)
    return level


def scatter_about(stream_key, shape, deviation, most, shards=(), kind=jnp.bfloat16):
    entries = deviation * jax.random.normal(stream_key, shape, jnp.float32)
    if shards:
        entries = entries * levels(stream_key, shape, shards, -0.22, 0.18)
    return jnp.clip(entries, -most, most).astype(kind)


def setup_inputs(seed: int = 0) -> dict:
    seeds = jax.random.split(jax.random.key(seed), 6)
    return {
        "green": scatter_about(seeds[0], (2, RECV, GRID), 1.0, 6.0, ((1, 32), (2, 8))),
        "source_weight": jnp.clip(jnp.exp(math.log(4.0) - 2.7725887 * jax.random.uniform(seeds[1], (GRID,), jnp.float32) ** levels(seeds[1], (GRID,), ((0, 8),), -0.2, 0.2)), 0.25, 4.0),
        "observed": scatter_about(seeds[2], (2, 2, RECV, NR), 1.0, 6.0, ((2, 32),), jnp.float32),
        "amp_weight": jnp.clip(jnp.exp(math.log(2.0) - 2.0794415 * jax.random.uniform(seeds[3], (2, RECV, NR), jnp.float32) ** levels(seeds[3], (2, RECV, NR), ((1, 32),), -0.2, 0.2)), 0.25, 2.0),
        "pair_used": place_ends((jax.random.randint(seeds[4], (NB, 2), 0, 4) < 3).astype(jnp.int32), jax.random.fold_in(seeds[4], 1), 0, 1),
    }


def build_block(resid_real, resid_imag):
    upper_half = jnp.concatenate([resid_real, resid_imag], axis=1)
    lower_half = jnp.concatenate([-resid_imag, resid_real], axis=1)
    return jnp.concatenate([upper_half, lower_half], axis=0)

def reference(green, source_weight, observed, amp_weight, pair_used):
    block_count = N_CABLE
    row_count = NR
    col_count = green.shape[2]
    inv_norm = 1.0 / math.sqrt(col_count)
    kernel_scale = inv_norm / (2.0 * math.sqrt(2.0 * block_count))
    stacked = green.reshape(2, block_count, row_count, col_count).transpose(1, 0, 2, 3).reshape(block_count, 2 * row_count, col_count)

    def one_block(index, state_pair):
        fields, kernel = state_pair
        own_block = stacked[index]
        weighted = (own_block.astype(jnp.float32) * source_weight[None, :]).astype(jnp.bfloat16)
        for offset in range(2):
            places = offset + 1
            earlier = (index - places) % block_count
            partner = stacked[earlier]
            products = lax.dot_general(weighted, partner, (((1,), (1,)), ((), ())), preferred_element_type=jnp.float32)
            corr_real = inv_norm * (products[:row_count, :row_count] + products[row_count:, row_count:])
            corr_imag = inv_norm * (products[:row_count, row_count:] - products[row_count:, :row_count])
            observed_rows = lax.dynamic_slice_in_dim(observed[offset], (index * row_count).astype(jnp.int32), row_count, 1)
            weight_rows = lax.dynamic_slice_in_dim(amp_weight[offset], (index * row_count).astype(jnp.int32), row_count, 0)
            mask_value = pair_used[index, offset].astype(jnp.float32)
            resid_real = (mask_value * weight_rows * (corr_real - observed_rows[0])).astype(jnp.bfloat16)
            resid_imag = (mask_value * weight_rows * (corr_imag - observed_rows[1])).astype(jnp.bfloat16)
            resid_block = build_block(resid_real, resid_imag)
            later_term = jnp.dot(resid_block, partner, preferred_element_type=jnp.float32)
            early_term = lax.dot_general(resid_block, own_block, (((0,), (0,)), ((), ())), preferred_element_type=jnp.float32)
            kernel = kernel + lax.optimization_barrier(jnp.sum(own_block.astype(jnp.float32) * later_term, axis=0))
            fields = fields.at[index].add(later_term)
            fields = fields.at[earlier].add(early_term)
        return (fields, kernel)
    fields = jnp.zeros((block_count, 2 * row_count, col_count), jnp.float32)
    kernel = jnp.zeros((col_count,), jnp.float32)
    fields, kernel = lax.fori_loop(0, block_count, one_block, (fields, kernel))
    fields = inv_norm * source_weight[None, None, :] * fields
    adjoint = fields.reshape(block_count, 2, row_count, col_count).transpose(1, 0, 2, 3).reshape(2, block_count * row_count, col_count)
    return (adjoint, kernel * kernel_scale)
```

```python
import math

import jax
import jax.numpy as jnp
from jax import lax
from jax.experimental import pallas as pl
from jax.experimental.pallas import tpu as pltpu
from jax.sharding import PartitionSpec as P


CHUNK = 512


def permuted(block, axis, source_of):
    size = lax.axis_size(axis)
    return lax.ppermute(block, axis, [(source_of(i) % size, i) for i in range(size)])


def partner(i):
    return i ^ 1


def near_chip(i):
    return i + 2 if i % 2 == 0 else i - 2


def far_chip(i):
    return i - 2 if i % 2 == 0 else i + 2


def corr_kernel(par, scale, own, mate, near, out, acc):
    step = pl.program_id(0)
    even = par[0] == 0
    own_cols = own[...]
    near_cols = near[...]
    earlier = jnp.where(even, own_cols, near_cols)
    for pair, later in enumerate((mate[...], jnp.where(even, near_cols, own_cols))):
        weighted = (later.astype(jnp.float32) * scale[...]).astype(jnp.bfloat16)
        products = lax.dot_general(
            weighted, earlier, (((1,), (1,)), ((), ())), preferred_element_type=jnp.float32
        )

        @pl.when(step == 0)
        def _():
            acc[pair] = products

        @pl.when(step > 0)
        def _():
            acc[pair] += products

    @pl.when(step == pl.num_programs(0) - 1)
    def _():
        parts, _, _, rows, cols = out.shape
        half = parts * rows
        for pair in range(2):
            real = acc[pair, :half, :half] + acc[pair, half:, half:]
            imag = acc[pair, :half, half:] - acc[pair, half:, :half]
            out[:, pair, 0] = real.reshape(parts, rows, cols)
            out[:, pair, 1] = imag.reshape(parts, rows, cols)


def field_kernel(inv_norm, par, scale, mine, mate_resid, far_resid, own, mate, mate_near, near, far, adjoint, kernel_part, mat):
    step = pl.program_id(0)
    parts, rows, cols = mine.shape[0], mine.shape[3], mine.shape[4]
    half = parts * rows

    def fill(position, real, imag, flip):
        real = real.reshape(half, cols)
        imag = imag.reshape(half, cols)
        if flip:
            real = real.astype(jnp.float32).T.astype(jnp.bfloat16)
            imag = (-imag.astype(jnp.float32)).T.astype(jnp.bfloat16)
        base = position * 2 * half
        mat[:half, base : base + half] = real
        mat[half:, base + half : base + 2 * half] = real
        mat[:half, base + half : base + 2 * half] = imag
        mat[half:, base : base + half] = -imag

    @pl.when((step == 0) & (par[0] == 0))
    def _():
        fill(0, mine[:, 0, 0], mine[:, 0, 1], True)
        fill(1, mate_resid[:, 0], mate_resid[:, 1], False)
        fill(2, mine[:, 1, 0], mine[:, 1, 1], True)
        fill(3, far_resid[:, 1, 0], far_resid[:, 1, 1], False)

    @pl.when((step == 0) & (par[0] == 1))
    def _():
        fill(0, mate_resid[:, 0], mate_resid[:, 1], False)
        fill(1, far_resid[:, 0, 0], far_resid[:, 0, 1], True)
        fill(2, mine[:, 1, 0], mine[:, 1, 1], False)
        fill(3, far_resid[:, 1, 0], far_resid[:, 1, 1], True)

    fields = None
    for position, block in enumerate((mate, mate_near, near, far)):
        term = jnp.dot(
            mat[:, position * 2 * half : (position + 1) * 2 * half], block[...], preferred_element_type=jnp.float32
        )
        fields = term if fields is None else fields + term
    kernel_part[...] = 0.5 * jnp.sum(own[...].astype(jnp.float32) * fields, axis=0, keepdims=True)
    adjoint[...] = (fields * (inv_norm * scale[...])).reshape(adjoint.shape)


def correlations(par, scale, own, mate, near, parts):
    both, cols = own.shape
    half = both // 2
    block = pl.BlockSpec((both, CHUNK), lambda j: (0, j))
    return pl.pallas_call(
        corr_kernel,
        out_shape=jax.ShapeDtypeStruct((parts, 2, 2, half // parts, half), jnp.float32),
        grid=(cols // CHUNK,),
        in_specs=[
            pl.BlockSpec(memory_space=pltpu.SMEM),
            pl.BlockSpec((1, CHUNK), lambda j: (0, j)),
            block,
            block,
            block,
        ],
        out_specs=pl.BlockSpec((parts, 2, 2, half // parts, half), lambda j: (0, 0, 0, 0, 0)),
        scratch_shapes=[pltpu.VMEM((2, both, both), jnp.float32)],
        cost_estimate=pl.CostEstimate(flops=4 * both * both * cols, bytes_accessed=8 * both * cols, transcendentals=0),
        compiler_params=pltpu.CompilerParams(vmem_limit_bytes=24 << 20),
        name="corr",
    )(par, scale, own, mate, near)


def fields_of(par, scale, mine, mate_resid, far_resid, own, mate, mate_near, near, far, inv_norm):
    both, cols = own.shape
    half = both // 2
    block = pl.BlockSpec((both, CHUNK), lambda j: (0, j))

    def whole(array):
        return pl.BlockSpec(array.shape, lambda j: (0,) * array.ndim)

    def body(*refs):
        field_kernel(inv_norm, *refs)

    return pl.pallas_call(
        body,
        out_shape=(
            jax.ShapeDtypeStruct((2, half, cols), jnp.float32),
            jax.ShapeDtypeStruct((1, cols), jnp.float32),
        ),
        grid=(cols // CHUNK,),
        in_specs=[
            pl.BlockSpec(memory_space=pltpu.SMEM),
            pl.BlockSpec((1, CHUNK), lambda j: (0, j)),
            whole(mine),
            whole(mate_resid),
            whole(far_resid),
            block,
            block,
            block,
            block,
            block,
        ],
        out_specs=(
            pl.BlockSpec((2, half, CHUNK), lambda j: (0, 0, j)),
            pl.BlockSpec((1, CHUNK), lambda j: (0, j)),
        ),
        scratch_shapes=[pltpu.VMEM((both, 4 * both), jnp.bfloat16)],
        cost_estimate=pl.CostEstimate(flops=8 * both * both * cols, bytes_accessed=18 * both * cols, transcendentals=0),
        compiler_params=pltpu.CompilerParams(vmem_limit_bytes=32 << 20),
        name="fields",
    )(par, scale, mine, mate_resid, far_resid, own, mate, mate_near, near, far)


def shards(green, source_weight, observed, amp_weight, pair_used):
    row_count, col_count = green.shape[1:]
    block_count = lax.axis_size("cable")
    parts = lax.axis_size("grid")
    inv_norm = 1.0 / math.sqrt(col_count * parts)
    kernel_scale = inv_norm / (2.0 * math.sqrt(2.0 * block_count))
    parity = lax.axis_index("cable") % 2
    par = parity.reshape(1)
    scale = source_weight[None, :]
    own = green.reshape(2 * row_count, col_count)

    near = permuted(own, "cable", near_chip)
    mate = permuted(own, "cable", partner)

    slice_rows = row_count // parts
    first = lax.axis_index("grid") * slice_rows
    observed_rows = lax.dynamic_slice_in_dim(observed, first, slice_rows, 2)
    weight_rows = lax.dynamic_slice_in_dim(amp_weight, first, slice_rows, 1)
    weight_rows = weight_rows * pair_used[0].astype(jnp.float32)[:, None, None]
    packed = jnp.concatenate([observed_rows, weight_rows[:, None]], axis=1)
    data_first = permuted(packed[0], "cable", partner)
    data_second = permuted(packed[1], "cable", near_chip)
    data_second = jnp.where(parity == 0, data_second, packed[1])
    data = jnp.stack([data_first, data_second])

    partials = correlations(par, scale, own, mate, near, parts)
    far = permuted(own, "cable", far_chip)
    mate_near = permuted(near, "cable", partner)
    pieces = lax.all_to_all(partials, "grid", 0, 0, tiled=True)
    corr = inv_norm * jnp.sum(pieces, axis=0)
    resid = (data[:, 2:] * (corr - data[:, :2])).astype(jnp.bfloat16)
    mine = lax.all_to_all(jnp.broadcast_to(resid[None], (parts,) + resid.shape), "grid", 0, 0, tiled=True)
    far_resid = permuted(mine, "cable", far_chip)
    mate_resid = permuted(mine[:, 0], "cable", partner)
    adjoint, kernel_part = fields_of(
        par, scale, mine, mate_resid, far_resid, own, mate, mate_near, near, far, inv_norm
    )
    kernel = kernel_part[0] * kernel_scale
    step = 1
    while step < block_count:
        kernel = kernel + permuted(kernel, "cable", lambda i: i ^ step)
        step *= 2
    return (adjoint, kernel)


def solution(mesh):
    in_specs = (
        P(None, "cable", "grid"),
        P("grid"),
        P(None, None, "cable", None),
        P(None, "cable", None),
        P("cable", None),
    )
    out_specs = (P(None, "cable", "grid"), P("grid"))

    return jax.shard_map(shards, mesh=mesh, in_specs=in_specs, out_specs=out_specs, check_vma=False)
```

```python
import math

import jax
import jax.numpy as jnp
from jax import lax
from jax.experimental import pallas as pl
from jax.experimental.pallas import tpu as pltpu
from jax.sharding import PartitionSpec as P


CHUNK = 512
HALVES = 2
WIRE = jnp.float32


def permuted(block, axis, source_of):
    size = lax.axis_size(axis)
    return lax.ppermute(block, axis, [(source_of(i) % size, i) for i in range(size)])


def partner(i):
    return i ^ 1


def near_chip(i):
    return i + 2 if i % 2 == 0 else i - 2


def far_chip(i):
    return i - 2 if i % 2 == 0 else i + 2


def whole(array):
    return pl.BlockSpec(array.shape, lambda j: (0,) * array.ndim)


def prep_kernel(par, used, first, observed, amp_weight, natural, second, square):
    rows = natural.shape[1]
    at = pl.ds(pl.multiple_of(first[0], rows), rows)
    masks = [used[0, o].astype(jnp.float32) for o in range(2)]
    natural[:2] = observed[0, :, at, :]
    natural[2] = amp_weight[0, at, :] * masks[0]

    @pl.when(par[0] == 0)
    def _():
        square[0] = observed[1, 0].T
        square[1] = -observed[1, 1].T
        square[2] = amp_weight[1].T * masks[1]
        second[...] = square[:, at, :]

    @pl.when(par[0] == 1)
    def _():
        second[:2] = observed[1, :, at, :]
        second[2] = amp_weight[1, at, :] * masks[1]


def prepared(par, used, first, observed, amp_weight, slice_rows):
    cols = amp_weight.shape[2]
    packed = (3, slice_rows, cols)
    smem = pl.BlockSpec(memory_space=pltpu.SMEM)
    return pl.pallas_call(
        prep_kernel,
        out_shape=(jax.ShapeDtypeStruct(packed, jnp.float32),) * 2,
        grid=(1,),
        in_specs=[smem, smem, smem, whole(observed), whole(amp_weight)],
        out_specs=(pl.BlockSpec(packed, lambda j: (0, 0, 0)),) * 2,
        scratch_shapes=[pltpu.VMEM((3, cols, cols), jnp.float32)],
        cost_estimate=pl.CostEstimate(flops=0, bytes_accessed=8 << 20, transcendentals=0),
        compiler_params=pltpu.CompilerParams(vmem_limit_bytes=8 << 20),
        name="prep",
    )(par, used, first, observed, amp_weight)


def resid_kernel(inv_norm, pieces, data, out):
    total = pieces[0].astype(jnp.float32)
    for part in range(1, pieces.shape[0]):
        total = total + pieces[part].astype(jnp.float32)
    resid = (data[:, 2:] * (inv_norm * total - data[:, :2])).astype(jnp.bfloat16)
    for part in range(out.shape[0]):
        out[part] = resid


def residuals(pieces, data, inv_norm, position):
    def body(*refs):
        resid_kernel(inv_norm, *refs)

    rows, cols = pieces.shape[3:]
    return pl.pallas_call(
        body,
        out_shape=jax.ShapeDtypeStruct(pieces.shape, jnp.bfloat16),
        grid=(1,),
        in_specs=[whole(pieces), pl.BlockSpec((2, 3, rows, cols), lambda j: (0, 0, 0, position))],
        out_specs=whole(pieces),
        cost_estimate=pl.CostEstimate(flops=0, bytes_accessed=2 << 20, transcendentals=0),
        compiler_params=pltpu.CompilerParams(vmem_limit_bytes=6 << 20),
        name="resid",
    )(pieces, data)


def corr_kernel(par, scale, lhs_first, lhs_second, own, near, out, acc):
    step = pl.program_id(0)
    even = par[0] == 0
    near_cols = near[...].reshape(-1, near.shape[2])
    rhs_first = jnp.where(even, own[...].reshape(near_cols.shape), near_cols)
    near_scale = jnp.where(even, scale[...], 1.0)
    rhs_second = (near_cols.astype(jnp.float32) * near_scale).astype(jnp.bfloat16)
    for pair, (lhs, rhs) in enumerate(((lhs_first, rhs_first), (lhs_second, rhs_second))):
        products = lax.dot_general(lhs[...], rhs, (((1,), (1,)), ((), ())), preferred_element_type=jnp.float32)

        @pl.when(step == 0)
        def _():
            acc[pair] = products

        @pl.when(step > 0)
        def _():
            acc[pair] += products

    @pl.when(step == pl.num_programs(0) - 1)
    def _():
        parts, _, _, rows, cols = out.shape
        half = parts * rows
        for pair in range(2):
            real = acc[pair, :half, :cols] + acc[pair, half:, cols:]
            imag = acc[pair, :half, cols:] - acc[pair, half:, :cols]
            out[:, pair, 0] = real.reshape(parts, rows, cols).astype(out.dtype)
            out[:, pair, 1] = imag.reshape(parts, rows, cols).astype(out.dtype)


def correlations(par, scale, lhs_first, lhs_second, green, near, parts, position):
    both, cols = lhs_first.shape
    half = both // 2
    part = half // HALVES
    lhs_block = pl.BlockSpec((both, CHUNK), lambda j: (0, j))
    out_shape = (parts, 2, 2, half // parts, part)
    return pl.pallas_call(
        corr_kernel,
        out_shape=jax.ShapeDtypeStruct(out_shape, WIRE),
        grid=(cols // CHUNK,),
        in_specs=[
            pl.BlockSpec(memory_space=pltpu.SMEM),
            pl.BlockSpec((1, CHUNK), lambda j: (0, j)),
            lhs_block,
            lhs_block,
            pl.BlockSpec((2, part, CHUNK), lambda j: (0, position, j)),
            pl.BlockSpec((2, part, CHUNK), lambda j: (0, 0, j)),
        ],
        out_specs=pl.BlockSpec(out_shape, lambda j: (0, 0, 0, 0, 0)),
        scratch_shapes=[pltpu.VMEM((2, both, 2 * part), jnp.float32)],
        cost_estimate=pl.CostEstimate(
            flops=8 * both * part * cols, bytes_accessed=4 * (both + part) * cols, transcendentals=0
        ),
        compiler_params=pltpu.CompilerParams(vmem_limit_bytes=20 << 20),
        name="corr",
    )(par, scale, lhs_first, lhs_second, green, near)


def assembled(pieces, pair, turned):
    square = []
    for component in range(2):
        strips = [piece[:, pair, component] for piece in pieces]
        strips = [strip.reshape(-1, strip.shape[-1]) for strip in strips]
        square.append(jnp.concatenate(strips, axis=1))
    real, imag = square
    if turned:
        real = real.astype(jnp.float32).T.astype(jnp.bfloat16)
        imag = (-imag.astype(jnp.float32)).T.astype(jnp.bfloat16)
    return real, imag


def place(mat, base, block, strips):
    real, imag = block
    half = real.shape[0]
    width = half // strips
    for strip in range(strips):
        x = real[:, strip * width : (strip + 1) * width]
        y = imag[:, strip * width : (strip + 1) * width]
        at = base + 2 * width * strip
        mat[:half, at : at + width] = x
        mat[half:, at + width : at + 2 * width] = x
        mat[:half, at + width : at + 2 * width] = y
        mat[half:, at : at + width] = -y


def applied(mat, base, pieces):
    total = None
    for piece in pieces:
        block = piece[...].reshape(-1, piece.shape[-1])
        term = jnp.dot(mat[:, base : base + block.shape[0]], block, preferred_element_type=jnp.float32)
        total = term if total is None else total + term
        base += block.shape[0]
    return total


def early_kernel(par, *refs):
    mine = refs[:HALVES]
    mate_resid = refs[HALVES : 2 * HALVES]
    own, mate = refs[2 * HALVES : 2 * HALVES + 2]
    near = refs[2 * HALVES + 2 : 3 * HALVES + 2]
    mate_near = refs[3 * HALVES + 2 : 4 * HALVES + 2]
    early, kernel_part, mat = refs[4 * HALVES + 2 :]
    first = pl.program_id(0) == 0
    even = par[0] == 0
    both = early.shape[0]

    @pl.when(first)
    def _():
        place(mat, 0, assembled(mine, 1, False), HALVES)

    @pl.when(first & even)
    def _():
        place(mat, both, assembled(mine, 0, True), 1)
        place(mat, 2 * both, assembled(mate_resid, 0, False), HALVES)

    @pl.when(first & jnp.logical_not(even))
    def _():
        place(mat, both, assembled(mate_resid, 0, False), 1)

    def finish(term):
        mate_term = applied(mat, both, (mate,))
        own_cols = own[...].astype(jnp.float32)
        kernel_part[...] = jnp.sum(own_cols * (term + 0.5 * mate_term), axis=0, keepdims=True)
        early[...] = term + mate_term

    @pl.when(even)
    def _():
        finish(applied(mat, 0, near) + applied(mat, 2 * both, mate_near))

    @pl.when(jnp.logical_not(even))
    def _():
        finish(applied(mat, 0, near))


def late_kernel(inv_norm, par, scale, *refs):
    far_resid = refs[:HALVES]
    far, early = refs[HALVES : HALVES + 2]
    mate_near = refs[HALVES + 2 : 2 * HALVES + 2]
    adjoint, mat = refs[2 * HALVES + 2 :]
    first = pl.program_id(0) == 0
    even = par[0] == 0
    both = early.shape[0]

    @pl.when(first)
    def _():
        place(mat, 0, assembled(far_resid, 1, True), 1)

    @pl.when(first & jnp.logical_not(even))
    def _():
        place(mat, both, assembled(far_resid, 0, True), HALVES)

    def finish(term):
        fields = early[...] + term
        adjoint[...] = (fields * (inv_norm * scale[...])).reshape(adjoint.shape)

    @pl.when(even)
    def _():
        finish(applied(mat, 0, (far,)))

    @pl.when(jnp.logical_not(even))
    def _():
        finish(applied(mat, 0, (far,)) + applied(mat, both, mate_near))


def column_block(array):
    shape = array.shape[:-1] + (CHUNK,)
    return pl.BlockSpec(shape, lambda j: (0,) * (array.ndim - 1) + (j,))


def early_fields(par, mine, mate_resid, own, mate, near, mate_near):
    both, cols = own.shape
    wholes = (*mine, *mate_resid)
    blocks = (own, mate, *near, *mate_near)
    return pl.pallas_call(
        early_kernel,
        out_shape=(
            jax.ShapeDtypeStruct((both, cols), jnp.float32),
            jax.ShapeDtypeStruct((1, cols), jnp.float32),
        ),
        grid=(cols // CHUNK,),
        in_specs=[pl.BlockSpec(memory_space=pltpu.SMEM)] + [whole(x) for x in wholes] + [column_block(x) for x in blocks],
        out_specs=(
            pl.BlockSpec((both, CHUNK), lambda j: (0, j)),
            pl.BlockSpec((1, CHUNK), lambda j: (0, j)),
        ),
        scratch_shapes=[pltpu.VMEM((both, 3 * both), jnp.bfloat16)],
        cost_estimate=pl.CostEstimate(flops=6 * both * both * cols, bytes_accessed=12 * both * cols, transcendentals=0),
        compiler_params=pltpu.CompilerParams(vmem_limit_bytes=24 << 20),
        name="early",
    )(par, *wholes, *blocks)


def late_fields(par, scale, far_resid, far, early, mate_near, inv_norm):
    both, cols = early.shape
    blocks = (far, early, *mate_near)

    def body(*refs):
        late_kernel(inv_norm, *refs)

    return pl.pallas_call(
        body,
        out_shape=jax.ShapeDtypeStruct((2, both // 2, cols), jnp.float32),
        grid=(cols // CHUNK,),
        in_specs=[pl.BlockSpec(memory_space=pltpu.SMEM), column_block(scale)]
        + [whole(x) for x in far_resid]
        + [column_block(x) for x in blocks],
        out_specs=pl.BlockSpec((2, both // 2, CHUNK), lambda j: (0, 0, j)),
        scratch_shapes=[pltpu.VMEM((both, 2 * both), jnp.bfloat16)],
        cost_estimate=pl.CostEstimate(flops=4 * both * both * cols, bytes_accessed=12 * both * cols, transcendentals=0),
        compiler_params=pltpu.CompilerParams(vmem_limit_bytes=24 << 20),
        name="late",
    )(par, scale, *far_resid, *blocks)


def shards(green, source_weight, observed, amp_weight, pair_used):
    row_count, col_count = green.shape[1:]
    block_count = lax.axis_size("cable")
    parts = lax.axis_size("grid")
    inv_norm = 1.0 / math.sqrt(col_count * parts)
    kernel_scale = inv_norm / (2.0 * math.sqrt(2.0 * block_count))
    parity = lax.axis_index("cable") % 2
    even = parity == 0
    par = parity.reshape(1)
    scale = source_weight[None, :]
    own = green.reshape(2 * row_count, col_count)
    width = row_count // HALVES

    near = []
    for half in range(HALVES):
        near.append(permuted(green[:, half * width : (half + 1) * width], "cable", near_chip))
    mate = permuted(own, "cable", partner)

    slice_rows = row_count // parts
    first = lax.axis_index("grid") * slice_rows
    packed = prepared(par, pair_used, first.reshape(1), observed, amp_weight, slice_rows)
    data_first = permuted(packed[0], "cable", partner)
    data_second = permuted(packed[1], "cable", near_chip)
    data = jnp.stack([data_first, jnp.where(even, data_second, packed[1])])

    lhs_first = (mate.astype(jnp.float32) * scale).astype(jnp.bfloat16)
    lhs_second = (own.astype(jnp.float32) * jnp.where(even, 1.0, scale)).astype(jnp.bfloat16)
    near[0], data, lhs_first, lhs_second = lax.optimization_barrier((near[0], data, lhs_first, lhs_second))

    partials = []
    for half in range(HALVES):
        partials.append(correlations(par, scale, lhs_first, lhs_second, green, near[half], parts, half))
    far = permuted(own, "cable", far_chip)
    mate_near = []
    for half in range(HALVES):
        mate_near.append(permuted(near[half], "cable", partner))
    mine, mate_resid, far_resid = [], [], []
    for half in range(HALVES):
        pieces = lax.all_to_all(partials[half], "grid", 0, 0, tiled=True)
        resid = residuals(pieces, data, inv_norm, half)
        gathered = lax.all_to_all(resid, "grid", 0, 0, tiled=True)
        mine.append(gathered)
        mate_resid.append(permuted(gathered[:, :1], "cable", partner))
        far_resid.append(permuted(gathered, "cable", far_chip))
    early, kernel_part = early_fields(par, mine, mate_resid, own, mate, near, mate_near)
    kernel = kernel_part[0] * kernel_scale
    adjoint = late_fields(par, scale, far_resid, far, early, mate_near, inv_norm)
    step = 1
    while step < block_count:
        kernel = kernel + permuted(kernel, "cable", lambda i: i ^ step)
        step *= 2
    return (adjoint, kernel)


def solution(mesh):
    in_specs = (
        P(None, "cable", "grid"),
        P("grid"),
        P(None, None, "cable", None),
        P(None, "cable", None),
        P("cable", None),
    )
    out_specs = (P(None, "cable", "grid"), P("grid"))

    return jax.shard_map(shards, mesh=mesh, in_specs=in_specs, out_specs=out_specs, check_vma=False)
```

```python
import math

import jax
import jax.numpy as jnp
from jax import lax
from jax.experimental import pallas as pl
from jax.experimental.pallas import tpu as pltpu
from jax.sharding import PartitionSpec as P


CHUNK = 512
WIRE = jnp.bfloat16


def permuted(block, axis, source_of):
    size = lax.axis_size(axis)
    return lax.ppermute(block, axis, [(source_of(i) % size, i) for i in range(size)])


def partner(i):
    return i ^ 1


def near_chip(i):
    return i + 2 if i % 2 == 0 else i - 2


def far_chip(i):
    return i - 2 if i % 2 == 0 else i + 2


def whole(array):
    return pl.BlockSpec(array.shape, lambda j: (0,) * array.ndim)


def prep_kernel(par, used, first, observed, amp_weight, natural, second, square):
    rows = natural.shape[1]
    at = pl.ds(pl.multiple_of(first[0], rows), rows)
    masks = [used[0, o].astype(jnp.float32) for o in range(2)]
    natural[:2] = observed[0, :, at, :]
    natural[2] = amp_weight[0, at, :] * masks[0]

    @pl.when(par[0] == 0)
    def _():
        square[0] = observed[1, 0].T
        square[1] = -observed[1, 1].T
        square[2] = amp_weight[1].T * masks[1]
        second[...] = square[:, at, :]

    @pl.when(par[0] == 1)
    def _():
        second[:2] = observed[1, :, at, :]
        second[2] = amp_weight[1, at, :] * masks[1]


def prepared(par, used, first, observed, amp_weight, slice_rows):
    cols = amp_weight.shape[2]
    packed = (3, slice_rows, cols)
    smem = pl.BlockSpec(memory_space=pltpu.SMEM)
    return pl.pallas_call(
        prep_kernel,
        out_shape=(jax.ShapeDtypeStruct(packed, jnp.float32),) * 2,
        grid=(1,),
        in_specs=[smem, smem, smem, whole(observed), whole(amp_weight)],
        out_specs=(pl.BlockSpec(packed, lambda j: (0, 0, 0)),) * 2,
        scratch_shapes=[pltpu.VMEM((3, cols, cols), jnp.float32)],
        cost_estimate=pl.CostEstimate(flops=0, bytes_accessed=8 << 20, transcendentals=0),
        compiler_params=pltpu.CompilerParams(vmem_limit_bytes=8 << 20),
        name="prep",
    )(par, used, first, observed, amp_weight)


def sum_kernel(pieces, total, wire):
    value = pieces[0].astype(jnp.float32)
    for part in range(1, pieces.shape[0]):
        value = value + pieces[part].astype(jnp.float32)
    total[...] = value
    wire[...] = value.astype(wire.dtype)


def summed(pieces):
    vmem = pl.BlockSpec(memory_space=pltpu.VMEM)
    shape = pieces.shape[1:]
    return pl.pallas_call(
        sum_kernel,
        out_shape=(jax.ShapeDtypeStruct(shape, jnp.float32), jax.ShapeDtypeStruct(shape, WIRE)),
        in_specs=[vmem],
        out_specs=(vmem, vmem),
        cost_estimate=pl.CostEstimate(flops=0, bytes_accessed=1 << 20, transcendentals=0),
        compiler_params=pltpu.CompilerParams(vmem_limit_bytes=4 << 20),
        name="summed",
    )(pieces)


def resid_kernel(inv_norm, total, other, data, out):
    corr = inv_norm * (total[...] + other[...].astype(jnp.float32))
    resid = (data[:, 2:] * (corr - data[:, :2])).astype(jnp.bfloat16)
    for part in range(out.shape[0]):
        out[part] = resid


def residuals(total, other, data, parts, inv_norm):
    def body(*refs):
        resid_kernel(inv_norm, *refs)

    vmem = pl.BlockSpec(memory_space=pltpu.VMEM)
    return pl.pallas_call(
        body,
        out_shape=jax.ShapeDtypeStruct((parts,) + total.shape, jnp.bfloat16),
        in_specs=[vmem] * 3,
        out_specs=vmem,
        cost_estimate=pl.CostEstimate(flops=0, bytes_accessed=2 << 20, transcendentals=0),
        compiler_params=pltpu.CompilerParams(vmem_limit_bytes=6 << 20),
        name="resid",
    )(total, other, data)


def corr_kernel(par, scale, lhs_first, lhs_second, own, near, out, acc):
    even = par[0] == 0
    acc[...] = jnp.zeros_like(acc)

    @pl.loop(0, own.shape[1] // CHUNK)
    def _(step):
        cols = pl.ds(pl.multiple_of(step * CHUNK, CHUNK), CHUNK)
        near_cols = near[:, cols]
        rhs_first = jnp.where(even, own[:, cols], near_cols)
        near_scale = jnp.where(even, scale[:, cols], 1.0)
        rhs_second = (near_cols.astype(jnp.float32) * near_scale).astype(jnp.bfloat16)
        for pair, (lhs, rhs) in enumerate(((lhs_first, rhs_first), (lhs_second, rhs_second))):
            acc[pair] += lax.dot_general(
                lhs[:, cols], rhs, (((1,), (1,)), ((), ())), preferred_element_type=jnp.float32
            )

    parts, _, _, rows, cols = out.shape
    half = parts * rows
    for pair in range(2):
        real = acc[pair, :half, :cols] + acc[pair, half:, cols:]
        imag = acc[pair, :half, cols:] - acc[pair, half:, :cols]
        out[:, pair, 0] = real.reshape(parts, rows, cols).astype(out.dtype)
        out[:, pair, 1] = imag.reshape(parts, rows, cols).astype(out.dtype)


def correlations(par, scale, lhs_first, lhs_second, own, near, parts):
    both, cols = own.shape
    half = both // 2
    vmem = pl.BlockSpec(memory_space=pltpu.VMEM)
    return pl.pallas_call(
        corr_kernel,
        out_shape=jax.ShapeDtypeStruct((parts, 2, 2, half // parts, half), WIRE),
        in_specs=[pl.BlockSpec(memory_space=pltpu.SMEM)] + [vmem] * 5,
        out_specs=vmem,
        scratch_shapes=[pltpu.VMEM((2, both, both), jnp.float32)],
        cost_estimate=pl.CostEstimate(flops=4 * both * both * cols, bytes_accessed=8 * both * cols, transcendentals=0),
        compiler_params=pltpu.CompilerParams(vmem_limit_bytes=24 << 20),
        name="corr",
    )(par, scale, lhs_first, lhs_second, own, near)


def assembled(gathered, pair, turned):
    real, imag = (gathered[:, pair, c].reshape(-1, gathered.shape[-1]) for c in range(2))
    if turned:
        real = real.astype(jnp.float32).T.astype(jnp.bfloat16)
        imag = (-imag.astype(jnp.float32)).T.astype(jnp.bfloat16)
    return real, imag


def place(mat, base, block):
    real, imag = block
    half = real.shape[0]
    mat[:half, base : base + half] = real
    mat[half:, base + half : base + 2 * half] = real
    mat[:half, base + half : base + 2 * half] = imag
    mat[half:, base : base + half] = -imag


def applied(mat, base, block):
    return jnp.dot(mat[:, base : base + block.shape[0]], block[...], preferred_element_type=jnp.float32)


def early_kernel(par, mine, mate_resid, own, mate, near, mate_near, early, kernel_part, mat):
    first = pl.program_id(0) == 0
    even = par[0] == 0
    both = early.shape[0]

    @pl.when(first)
    def _():
        place(mat, 0, assembled(mine, 1, False))

    @pl.when(first & even)
    def _():
        place(mat, both, assembled(mine, 0, True))
        place(mat, 2 * both, assembled(mate_resid, 0, False))

    @pl.when(first & jnp.logical_not(even))
    def _():
        place(mat, both, assembled(mate_resid, 0, False))

    def finish(term):
        mate_term = applied(mat, both, mate)
        own_cols = own[...].astype(jnp.float32)
        kernel_part[...] = jnp.sum(own_cols * (term + 0.5 * mate_term), axis=0, keepdims=True)
        early[...] = term + mate_term

    @pl.when(even)
    def _():
        finish(applied(mat, 0, near) + applied(mat, 2 * both, mate_near))

    @pl.when(jnp.logical_not(even))
    def _():
        finish(applied(mat, 0, near))


def late_kernel(inv_norm, par, scale, far_resid, far, early, mate_near, adjoint, mat):
    first = pl.program_id(0) == 0
    even = par[0] == 0
    both = early.shape[0]

    @pl.when(first)
    def _():
        place(mat, 0, assembled(far_resid, 1, True))

    @pl.when(first & jnp.logical_not(even))
    def _():
        place(mat, both, assembled(far_resid, 0, True))

    def finish(term):
        fields = early[...] + term
        adjoint[...] = (fields * (inv_norm * scale[...])).reshape(adjoint.shape)

    @pl.when(even)
    def _():
        finish(applied(mat, 0, far))

    @pl.when(jnp.logical_not(even))
    def _():
        finish(applied(mat, 0, far) + applied(mat, both, mate_near))


def column_block(array):
    shape = array.shape[:-1] + (CHUNK,)
    return pl.BlockSpec(shape, lambda j: (0,) * (array.ndim - 1) + (j,))


def early_fields(par, mine, mate_resid, own, mate, near, mate_near):
    both, cols = own.shape
    wholes = (mine, mate_resid)
    blocks = (own, mate, near, mate_near)
    return pl.pallas_call(
        early_kernel,
        out_shape=(
            jax.ShapeDtypeStruct((both, cols), jnp.float32),
            jax.ShapeDtypeStruct((1, cols), jnp.float32),
        ),
        grid=(cols // CHUNK,),
        in_specs=[pl.BlockSpec(memory_space=pltpu.SMEM)] + [whole(x) for x in wholes] + [column_block(x) for x in blocks],
        out_specs=(
            pl.BlockSpec((both, CHUNK), lambda j: (0, j)),
            pl.BlockSpec((1, CHUNK), lambda j: (0, j)),
        ),
        scratch_shapes=[pltpu.VMEM((both, 3 * both), jnp.bfloat16)],
        cost_estimate=pl.CostEstimate(flops=6 * both * both * cols, bytes_accessed=12 * both * cols, transcendentals=0),
        compiler_params=pltpu.CompilerParams(vmem_limit_bytes=24 << 20),
        name="early",
    )(par, *wholes, *blocks)


def late_fields(par, scale, far_resid, far, early, mate_near, inv_norm):
    both, cols = early.shape
    blocks = (far, early, mate_near)

    def body(*refs):
        late_kernel(inv_norm, *refs)

    return pl.pallas_call(
        body,
        out_shape=jax.ShapeDtypeStruct((2, both // 2, cols), jnp.float32),
        grid=(cols // CHUNK,),
        in_specs=[pl.BlockSpec(memory_space=pltpu.SMEM), column_block(scale)]
        + [whole(far_resid)]
        + [column_block(x) for x in blocks],
        out_specs=pl.BlockSpec((2, both // 2, CHUNK), lambda j: (0, 0, j)),
        scratch_shapes=[pltpu.VMEM((both, 2 * both), jnp.bfloat16)],
        cost_estimate=pl.CostEstimate(flops=4 * both * both * cols, bytes_accessed=12 * both * cols, transcendentals=0),
        compiler_params=pltpu.CompilerParams(vmem_limit_bytes=24 << 20),
        name="late",
    )(par, scale, far_resid, *blocks)


def shards(green, source_weight, observed, amp_weight, pair_used):
    row_count, col_count = green.shape[1:]
    block_count = lax.axis_size("cable")
    parts = lax.axis_size("grid")
    inv_norm = 1.0 / math.sqrt(col_count * parts)
    kernel_scale = inv_norm / (2.0 * math.sqrt(2.0 * block_count))
    parity = lax.axis_index("cable") % 2
    even = parity == 0
    par = parity.reshape(1)
    scale = source_weight[None, :]
    own = green.reshape(2 * row_count, col_count)
    pieces_count = parts // 2
    along_x = [list(range(i, parts, 2)) for i in range(2)]

    near = permuted(own, "cable", near_chip)
    mate = permuted(own, "cable", partner)

    slice_rows = row_count // pieces_count
    first = lax.axis_index("grid") // 2 * slice_rows
    packed = prepared(par, pair_used, first.reshape(1), observed, amp_weight, slice_rows)
    data_first = permuted(packed[0], "cable", partner)
    data_second = permuted(packed[1], "cable", near_chip)
    data = jnp.stack([data_first, jnp.where(even, data_second, packed[1])])

    lhs_first = (mate.astype(jnp.float32) * scale).astype(jnp.bfloat16)
    lhs_second = (own.astype(jnp.float32) * jnp.where(even, 1.0, scale)).astype(jnp.bfloat16)
    near, data, lhs_first, lhs_second = lax.optimization_barrier((near, data, lhs_first, lhs_second))

    partials = correlations(par, scale, lhs_first, lhs_second, own, near, pieces_count)
    far = permuted(own, "cable", far_chip)
    mate_near = permuted(near, "cable", partner)
    pieces = lax.all_to_all(partials, "grid", 0, 0, tiled=True, axis_index_groups=along_x)
    total, wire = summed(pieces)
    other = permuted(wire, "grid", partner)
    resid = residuals(total, other, data, pieces_count, inv_norm)
    mine = lax.all_to_all(resid, "grid", 0, 0, tiled=True, axis_index_groups=along_x)
    mate_resid = permuted(mine[:, :1], "cable", partner)
    far_resid = permuted(mine, "cable", far_chip)
    early, kernel_part = early_fields(par, mine, mate_resid, own, mate, near, mate_near)
    kernel = kernel_part[0] * kernel_scale
    adjoint = late_fields(par, scale, far_resid, far, early, mate_near, inv_norm)
    distance = block_count // 2
    swapped = [permuted(kernel, "cable", lambda i: i ^ d) for d in (1, distance, distance + 1)]
    kernel = (kernel + swapped[0]) + (swapped[1] + swapped[2])
    step = 2
    while step < distance:
        kernel = kernel + permuted(kernel, "cable", lambda i: i ^ step)
        step *= 2
    return (adjoint, kernel)


def solution(mesh):
    in_specs = (
        P(None, "cable", "grid"),
        P("grid"),
        P(None, None, "cable", None),
        P(None, "cable", None),
        P("cable", None),
    )
    out_specs = (P(None, "cable", "grid"), P("grid"))

    return jax.shard_map(shards, mesh=mesh, in_specs=in_specs, out_specs=out_specs, check_vma=False)
```

```python
import math

import jax
import jax.numpy as jnp
from jax import lax
from jax.experimental import pallas as pl
from jax.experimental.pallas import tpu as pltpu
from jax.sharding import PartitionSpec as P


CHUNK = 512
WIRE = jnp.bfloat16


def permuted(block, axis, source_of):
    size = lax.axis_size(axis)
    return lax.ppermute(block, axis, [(source_of(i) % size, i) for i in range(size)])


def partner(i):
    return i ^ 1


def near_chip(i):
    return i + 2 if i % 2 == 0 else i - 2


def far_chip(i):
    return i - 2 if i % 2 == 0 else i + 2


def whole(array):
    return pl.BlockSpec(array.shape, lambda j: (0,) * array.ndim)


def prep_kernel(par, used, first, observed, amp_weight, natural, second, square):
    rows = natural.shape[1]
    at = pl.ds(pl.multiple_of(first[0], rows), rows)
    masks = [used[0, o].astype(jnp.float32) for o in range(2)]
    natural[:2] = observed[0, :, at, :]
    natural[2] = amp_weight[0, at, :] * masks[0]

    @pl.when(par[0] == 0)
    def _():
        square[0] = observed[1, 0].T
        square[1] = -observed[1, 1].T
        square[2] = amp_weight[1].T * masks[1]
        second[...] = square[:, at, :]

    @pl.when(par[0] == 1)
    def _():
        second[:2] = observed[1, :, at, :]
        second[2] = amp_weight[1, at, :] * masks[1]


def prepared(par, used, first, observed, amp_weight, slice_rows):
    cols = amp_weight.shape[2]
    packed = (3, slice_rows, cols)
    smem = pl.BlockSpec(memory_space=pltpu.SMEM)
    return pl.pallas_call(
        prep_kernel,
        out_shape=(jax.ShapeDtypeStruct(packed, jnp.float32),) * 2,
        grid=(1,),
        in_specs=[smem, smem, smem, whole(observed), whole(amp_weight)],
        out_specs=(pl.BlockSpec(packed, lambda j: (0, 0, 0)),) * 2,
        scratch_shapes=[pltpu.VMEM((3, cols, cols), jnp.float32)],
        cost_estimate=pl.CostEstimate(flops=0, bytes_accessed=8 << 20, transcendentals=0),
        compiler_params=pltpu.CompilerParams(vmem_limit_bytes=8 << 20),
        name="prep",
    )(par, used, first, observed, amp_weight)


def sum_kernel(pieces, total, wire):
    value = pieces[0].astype(jnp.float32)
    for part in range(1, pieces.shape[0]):
        value = value + pieces[part].astype(jnp.float32)
    total[...] = value
    wire[...] = value.astype(wire.dtype)


def summed(pieces):
    vmem = pl.BlockSpec(memory_space=pltpu.VMEM)
    shape = pieces.shape[1:]
    return pl.pallas_call(
        sum_kernel,
        out_shape=(jax.ShapeDtypeStruct(shape, jnp.float32), jax.ShapeDtypeStruct(shape, WIRE)),
        in_specs=[vmem],
        out_specs=(vmem, vmem),
        cost_estimate=pl.CostEstimate(flops=0, bytes_accessed=1 << 20, transcendentals=0),
        compiler_params=pltpu.CompilerParams(vmem_limit_bytes=4 << 20),
        name="summed",
    )(pieces)


def resid_kernel(inv_norm, total, other, data, out):
    corr = inv_norm * (total[...] + other[...].astype(jnp.float32))
    resid = (data[:, 2:] * (corr - data[:, :2])).astype(jnp.bfloat16)
    for part in range(out.shape[0]):
        out[part] = resid


def residuals(total, other, data, parts, inv_norm):
    def body(*refs):
        resid_kernel(inv_norm, *refs)

    vmem = pl.BlockSpec(memory_space=pltpu.VMEM)
    return pl.pallas_call(
        body,
        out_shape=jax.ShapeDtypeStruct((parts,) + total.shape, jnp.bfloat16),
        in_specs=[vmem] * 3,
        out_specs=vmem,
        cost_estimate=pl.CostEstimate(flops=0, bytes_accessed=2 << 20, transcendentals=0),
        compiler_params=pltpu.CompilerParams(vmem_limit_bytes=6 << 20),
        name="resid",
    )(total, other, data)


def corr_kernel(par, scale, lhs_first, lhs_second, own, near, out, acc):
    even = par[0] == 0
    acc[...] = jnp.zeros_like(acc)

    @pl.loop(0, own.shape[1] // CHUNK)
    def _(step):
        cols = pl.ds(pl.multiple_of(step * CHUNK, CHUNK), CHUNK)
        near_cols = near[:, cols]
        rhs_first = jnp.where(even, own[:, cols], near_cols)
        near_scale = jnp.where(even, scale[:, cols], 1.0)
        rhs_second = (near_cols.astype(jnp.float32) * near_scale).astype(jnp.bfloat16)
        for pair, (lhs, rhs) in enumerate(((lhs_first, rhs_first), (lhs_second, rhs_second))):
            acc[pair] += lax.dot_general(
                lhs[:, cols], rhs, (((1,), (1,)), ((), ())), preferred_element_type=jnp.float32
            )

    parts, _, _, rows, cols = out.shape
    half = parts * rows
    for pair in range(2):
        real = acc[pair, :half, :cols] + acc[pair, half:, cols:]
        imag = acc[pair, :half, cols:] - acc[pair, half:, :cols]
        out[:, pair, 0] = real.reshape(parts, rows, cols).astype(out.dtype)
        out[:, pair, 1] = imag.reshape(parts, rows, cols).astype(out.dtype)


def correlations(par, scale, lhs_first, lhs_second, own, near, parts):
    both, cols = own.shape
    half = both // 2
    vmem = pl.BlockSpec(memory_space=pltpu.VMEM)
    return pl.pallas_call(
        corr_kernel,
        out_shape=jax.ShapeDtypeStruct((parts, 2, 2, half // parts, half), WIRE),
        in_specs=[pl.BlockSpec(memory_space=pltpu.SMEM)] + [vmem] * 5,
        out_specs=vmem,
        scratch_shapes=[pltpu.VMEM((2, both, both), jnp.float32)],
        cost_estimate=pl.CostEstimate(flops=4 * both * both * cols, bytes_accessed=8 * both * cols, transcendentals=0),
        compiler_params=pltpu.CompilerParams(vmem_limit_bytes=24 << 20),
        name="corr",
    )(par, scale, lhs_first, lhs_second, own, near)


def assembled(gathered, pair, turned):
    real, imag = (gathered[:, pair, c].reshape(-1, gathered.shape[-1]) for c in range(2))
    if turned:
        real = real.astype(jnp.float32).T.astype(jnp.bfloat16)
        imag = (-imag.astype(jnp.float32)).T.astype(jnp.bfloat16)
    return real, imag


def place(mat, base, block):
    real, imag = block
    half = real.shape[0]
    mat[:half, base : base + half] = real
    mat[half:, base + half : base + 2 * half] = real
    mat[:half, base + half : base + 2 * half] = imag
    mat[half:, base : base + half] = -imag


def applied(mat, base, block):
    return jnp.dot(mat[:, base : base + block.shape[0]], block[...], preferred_element_type=jnp.float32)


def early_kernel(par, mine, mate_resid, own, mate, near, mate_near, early, kernel_part, mat):
    both = early.shape[0]

    @pl.when(pl.program_id(0) == 0)
    def _():
        place(mat, 0, assembled(mine, 1, False))
        place(mat, both, assembled(mate_resid, 0, False))

    second = jnp.where(par[0] == 0, mate_near[...], mate[...])
    fields = applied(mat, 0, near) + applied(mat, both, second)
    kernel_part[...] = jnp.sum(own[...].astype(jnp.float32) * fields, axis=0, keepdims=True)
    early[...] = fields


def late_kernel(inv_norm, par, scale, mine, far_resid, far_real, far_imag, early, mate, mate_near, adjoint, mat):
    first = pl.program_id(0) == 0
    even = par[0] == 0
    both = early.shape[0]

    @pl.when(first)
    def _():
        place(mat, 0, assembled(far_resid, 1, True))

    @pl.when(first & even)
    def _():
        place(mat, both, assembled(mine, 0, True))

    @pl.when(first & jnp.logical_not(even))
    def _():
        place(mat, both, assembled(far_resid, 0, True))

    second = jnp.where(even, mate[...], mate_near[...])
    term = applied(mat, 0, far_real) + applied(mat, both // 2, far_imag) + applied(mat, both, second)
    adjoint[...] = ((early[...] + term) * (inv_norm * scale[...])).reshape(adjoint.shape)


def ring_kernel(place_of, rows, above, below, out, slots):
    count = slots.shape[0]
    position = 0
    for piece, offset in ((below, -3), (rows, -1), (above, 2)):
        for i in range(piece.shape[0]):
            slots[lax.rem(place_of[0] + (offset + i + count), count)] = piece[i]
            position += 1
    assert position == count
    total = slots[0]
    for i in range(1, count):
        total = total + slots[i]
    out[...] = total


def ring_sum(place_of, rows, above, below, count):
    vmem = pl.BlockSpec(memory_space=pltpu.VMEM)
    return pl.pallas_call(
        ring_kernel,
        out_shape=jax.ShapeDtypeStruct(rows.shape[1:], jnp.float32),
        in_specs=[pl.BlockSpec(memory_space=pltpu.SMEM)] + [vmem] * 3,
        out_specs=vmem,
        scratch_shapes=[pltpu.VMEM((count,) + rows.shape[1:], jnp.float32)],
        cost_estimate=pl.CostEstimate(flops=0, bytes_accessed=1 << 17, transcendentals=0),
        compiler_params=pltpu.CompilerParams(vmem_limit_bytes=1 << 20),
        name="ring_sum",
    )(place_of, rows, above, below)


def column_block(array):
    shape = array.shape[:-1] + (CHUNK,)
    return pl.BlockSpec(shape, lambda j: (0,) * (array.ndim - 1) + (j,))


def early_fields(par, mine, mate_resid, own, mate, near, mate_near):
    both, cols = own.shape
    wholes = (mine, mate_resid)
    blocks = (own, mate, near, mate_near)
    return pl.pallas_call(
        early_kernel,
        out_shape=(
            pltpu.HBM((both, cols), jnp.float32),
            jax.ShapeDtypeStruct((1, cols), jnp.float32),
        ),
        grid=(cols // CHUNK,),
        in_specs=[pl.BlockSpec(memory_space=pltpu.SMEM)] + [whole(x) for x in wholes] + [column_block(x) for x in blocks],
        out_specs=(
            pl.BlockSpec((both, CHUNK), lambda j: (0, j)),
            pl.BlockSpec((1, CHUNK), lambda j: (0, j)),
        ),
        scratch_shapes=[pltpu.VMEM((both, 2 * both), jnp.bfloat16)],
        cost_estimate=pl.CostEstimate(flops=4 * both * both * cols, bytes_accessed=12 * both * cols, transcendentals=0),
        compiler_params=pltpu.CompilerParams(vmem_limit_bytes=24 << 20),
        name="early",
    )(par, *wholes, *blocks)


def late_fields(par, scale, mine, far_resid, far, early, mate, mate_near, inv_norm):
    both, cols = early.shape
    blocks = (*far, early, mate, mate_near)

    def body(*refs):
        late_kernel(inv_norm, *refs)

    return pl.pallas_call(
        body,
        out_shape=jax.ShapeDtypeStruct((2, both // 2, cols), jnp.float32),
        grid=(cols // CHUNK,),
        in_specs=[pl.BlockSpec(memory_space=pltpu.SMEM), column_block(scale)]
        + [whole(mine), whole(far_resid)]
        + [column_block(x) for x in blocks],
        out_specs=pl.BlockSpec((2, both // 2, CHUNK), lambda j: (0, 0, j)),
        scratch_shapes=[pltpu.VMEM((both, 2 * both), jnp.bfloat16)],
        cost_estimate=pl.CostEstimate(flops=4 * both * both * cols, bytes_accessed=12 * both * cols, transcendentals=0),
        compiler_params=pltpu.CompilerParams(vmem_limit_bytes=24 << 20),
        name="late",
    )(par, scale, mine, far_resid, *blocks)


def shards(green, source_weight, observed, amp_weight, pair_used):
    row_count, col_count = green.shape[1:]
    block_count = lax.axis_size("cable")
    parts = lax.axis_size("grid")
    inv_norm = 1.0 / math.sqrt(col_count * parts)
    kernel_scale = inv_norm / (2.0 * math.sqrt(2.0 * block_count))
    parity = lax.axis_index("cable") % 2
    even = parity == 0
    par = parity.reshape(1)
    scale = source_weight[None, :]
    own = green.reshape(2 * row_count, col_count)
    pieces_count = parts // 2
    along_x = [list(range(i, parts, 2)) for i in range(2)]

    near = permuted(own, "cable", near_chip)
    mate = permuted(own, "cable", partner)

    slice_rows = row_count // pieces_count
    first = lax.axis_index("grid") // 2 * slice_rows
    packed = prepared(par, pair_used, first.reshape(1), observed, amp_weight, slice_rows)
    data_first = permuted(packed[0], "cable", partner)
    data_second = permuted(packed[1], "cable", near_chip)
    data = jnp.stack([data_first, jnp.where(even, data_second, packed[1])])

    lhs_first = (mate.astype(jnp.float32) * scale).astype(jnp.bfloat16)
    lhs_second = (own.astype(jnp.float32) * jnp.where(even, 1.0, scale)).astype(jnp.bfloat16)
    cuts = (green[0], green[1])
    near, lhs_first, lhs_second, cuts = lax.optimization_barrier((near, lhs_first, lhs_second, cuts))

    partials = correlations(par, scale, lhs_first, lhs_second, own, near, pieces_count)
    far = []
    for component in range(2):
        far.append(permuted(cuts[component], "cable", far_chip))
    mate_near = permuted(near, "cable", partner)
    pieces = lax.all_to_all(partials, "grid", 0, 0, tiled=True, axis_index_groups=along_x)
    total, wire = summed(pieces)
    other = permuted(wire, "grid", partner)
    resid = residuals(total, other, data, pieces_count, inv_norm)
    mine = lax.all_to_all(resid, "grid", 0, 0, tiled=True, axis_index_groups=along_x)
    mate_resid = permuted(mine[:, :1], "cable", partner)
    far_resid = permuted(mine, "cable", far_chip)
    early, kernel_part = early_fields(par, mine, mate_resid, own, mate, near, mate_near)
    kernel = kernel_part[0] * kernel_scale
    adjoint = late_fields(par, scale, mine, far_resid, far, early, mate, mate_near, inv_norm)
    distance = block_count // 2
    swapped = [permuted(kernel, "cable", lambda i: i ^ d) for d in (1, distance, distance + 1)]
    kernel = (kernel + swapped[0]) + (swapped[1] + swapped[2])

    def along_z(hops):
        return lambda i: i // distance * distance + (i + 2 * hops) % distance

    kernel = kernel.reshape(1, 16, -1)
    neighbours = [permuted(kernel, "cable", along_z(hops)) for hops in (-1, 1)]
    rows = jnp.concatenate([neighbours[0], kernel, neighbours[1]], axis=0)
    above = permuted(rows, "cable", along_z(3))
    below = permuted(rows[1:], "cable", along_z(-3))
    place_of = lax.axis_index("cable") % distance // 2
    kernel = ring_sum(place_of.reshape(1), rows, above, below, distance // 2).reshape(col_count)
    return (adjoint, kernel)


def solution(mesh):
    in_specs = (
        P(None, "cable", "grid"),
        P("grid"),
        P(None, None, "cable", None),
        P(None, "cable", None),
        P("cable", None),
    )
    out_specs = (P(None, "cable", "grid"), P("grid"))

    return jax.shard_map(shards, mesh=mesh, in_specs=in_specs, out_specs=out_specs, check_vma=False)
```

```python
import math

import jax
import jax.numpy as jnp
from jax import lax
from jax.experimental import pallas as pl
from jax.experimental.pallas import tpu as pltpu
from jax.sharding import PartitionSpec as P


CHUNK = 512
WIRE = jnp.bfloat16


def permuted(block, axis, source_of):
    size = lax.axis_size(axis)
    return lax.ppermute(block, axis, [(source_of(i) % size, i) for i in range(size)])


def partner(i):
    return i ^ 1


def near_chip(i):
    return i + 2 if i % 2 == 0 else i - 2


def far_chip(i):
    return i - 2 if i % 2 == 0 else i + 2


def whole(array):
    return pl.BlockSpec(array.shape, lambda j: (0,) * array.ndim)


def prep_kernel(par, used, first, observed, amp_weight, natural, second, square):
    rows = natural.shape[1]
    at = pl.ds(pl.multiple_of(first[0], rows), rows)
    masks = [used[0, o].astype(jnp.float32) for o in range(2)]
    natural[:2] = observed[0, :, at, :]
    natural[2] = amp_weight[0, at, :] * masks[0]

    @pl.when(par[0] == 0)
    def _():
        square[0] = observed[1, 0].T
        square[1] = -observed[1, 1].T
        square[2] = amp_weight[1].T * masks[1]
        second[...] = square[:, at, :]

    @pl.when(par[0] == 1)
    def _():
        second[:2] = observed[1, :, at, :]
        second[2] = amp_weight[1, at, :] * masks[1]


def prepared(par, used, first, observed, amp_weight, slice_rows):
    cols = amp_weight.shape[2]
    packed = (3, slice_rows, cols)
    smem = pl.BlockSpec(memory_space=pltpu.SMEM)
    return pl.pallas_call(
        prep_kernel,
        out_shape=(jax.ShapeDtypeStruct(packed, jnp.float32),) * 2,
        grid=(1,),
        in_specs=[smem, smem, smem, whole(observed), whole(amp_weight)],
        out_specs=(pl.BlockSpec(packed, lambda j: (0, 0, 0)),) * 2,
        scratch_shapes=[pltpu.VMEM((3, cols, cols), jnp.float32)],
        cost_estimate=pl.CostEstimate(flops=0, bytes_accessed=8 << 20, transcendentals=0),
        compiler_params=pltpu.CompilerParams(vmem_limit_bytes=8 << 20),
        name="prep",
    )(par, used, first, observed, amp_weight)


def sum_kernel(pieces, total, wire):
    value = pieces[0].astype(jnp.float32)
    for part in range(1, pieces.shape[0]):
        value = value + pieces[part].astype(jnp.float32)
    total[...] = value
    wire[...] = value.astype(wire.dtype)


def summed(pieces):
    vmem = pl.BlockSpec(memory_space=pltpu.VMEM)
    shape = pieces.shape[1:]
    return pl.pallas_call(
        sum_kernel,
        out_shape=(jax.ShapeDtypeStruct(shape, jnp.float32), jax.ShapeDtypeStruct(shape, WIRE)),
        in_specs=[vmem],
        out_specs=(vmem, vmem),
        cost_estimate=pl.CostEstimate(flops=0, bytes_accessed=1 << 20, transcendentals=0),
        compiler_params=pltpu.CompilerParams(vmem_limit_bytes=4 << 20),
        name="summed",
    )(pieces)


def resid_kernel(inv_norm, total, other, data, out):
    corr = inv_norm * (total[...] + other[...].astype(jnp.float32))
    resid = (data[:, 2:] * (corr - data[:, :2])).astype(jnp.bfloat16)
    for part in range(out.shape[0]):
        out[part] = resid


def residuals(total, other, data, parts, inv_norm):
    def body(*refs):
        resid_kernel(inv_norm, *refs)

    vmem = pl.BlockSpec(memory_space=pltpu.VMEM)
    return pl.pallas_call(
        body,
        out_shape=jax.ShapeDtypeStruct((parts,) + total.shape, jnp.bfloat16),
        in_specs=[vmem] * 3,
        out_specs=vmem,
        cost_estimate=pl.CostEstimate(flops=0, bytes_accessed=2 << 20, transcendentals=0),
        compiler_params=pltpu.CompilerParams(vmem_limit_bytes=6 << 20),
        name="resid",
    )(total, other, data)


def fetches(pairs, sems):
    chunks = pairs[0][1].shape[1] // CHUNK
    copies = []
    for j in range(chunks):
        cols = pl.ds(j * CHUNK, CHUNK)
        row = []
        for i, (source, target) in enumerate(pairs):
            copy = pltpu.make_async_copy(source.at[:, cols], target.at[:, cols], sems.at[i, j])
            copy.start()
            row.append(copy)
        copies.append(row)
    return copies


def corr_kernel(par, scale, lhs_first, lhs_second, own, near_source, out, acc, near, sems):
    even = par[0] == 0
    for j, copies in enumerate(fetches([(near_source, near)], sems)):
        for copy in copies:
            copy.wait()
        cols = pl.ds(j * CHUNK, CHUNK)
        near_cols = near[:, cols]
        rhs_first = jnp.where(even, own[:, cols], near_cols)
        near_scale = jnp.where(even, scale[:, cols], 1.0)
        rhs_second = (near_cols.astype(jnp.float32) * near_scale).astype(jnp.bfloat16)
        for pair, (lhs, rhs) in enumerate(((lhs_first, rhs_first), (lhs_second, rhs_second))):
            products = lax.dot_general(
                lhs[:, cols], rhs, (((1,), (1,)), ((), ())), preferred_element_type=jnp.float32
            )
            if j == 0:
                acc[pair] = products
            else:
                acc[pair] += products

    parts, _, _, rows, cols = out.shape
    half = parts * rows
    for pair in range(2):
        real = acc[pair, :half, :cols] + acc[pair, half:, cols:]
        imag = acc[pair, :half, cols:] - acc[pair, half:, :cols]
        out[:, pair, 0] = real.reshape(parts, rows, cols).astype(out.dtype)
        out[:, pair, 1] = imag.reshape(parts, rows, cols).astype(out.dtype)


def correlations(par, scale, lhs_first, lhs_second, own, near, parts):
    both, cols = own.shape
    half = both // 2
    vmem = pl.BlockSpec(memory_space=pltpu.VMEM)
    return pl.pallas_call(
        corr_kernel,
        out_shape=jax.ShapeDtypeStruct((parts, 2, 2, half // parts, half), WIRE),
        in_specs=[pl.BlockSpec(memory_space=pltpu.SMEM)] + [vmem] * 4 + [pl.BlockSpec(memory_space=pl.ANY)],
        out_specs=vmem,
        scratch_shapes=[
            pltpu.VMEM((2, both, both), jnp.float32),
            pltpu.VMEM((both, cols), jnp.bfloat16),
            pltpu.SemaphoreType.DMA((1, cols // CHUNK)),
        ],
        cost_estimate=pl.CostEstimate(flops=4 * both * both * cols, bytes_accessed=8 * both * cols, transcendentals=0),
        compiler_params=pltpu.CompilerParams(vmem_limit_bytes=24 << 20),
        name="corr",
    )(par, scale, lhs_first, lhs_second, own, near)


def assembled(gathered, pair, turned):
    real, imag = (gathered[:, pair, c].reshape(-1, gathered.shape[-1]) for c in range(2))
    if turned:
        real = real.astype(jnp.float32).T.astype(jnp.bfloat16)
        imag = (-imag.astype(jnp.float32)).T.astype(jnp.bfloat16)
    return real, imag


def place(mat, base, block):
    real, imag = block
    half = real.shape[0]
    mat[:half, base : base + half] = real
    mat[half:, base + half : base + 2 * half] = real
    mat[:half, base + half : base + 2 * half] = imag
    mat[half:, base : base + half] = -imag


def early_kernel(par, mine, mate_resid, own_source, mate_source, near_source, mate_near_source, early, kernel_part, mat, own, second, near, out, sems, out_sems):
    both = early.shape[0]

    def run(second_source):
        copies = fetches([(near_source, near), (second_source, second), (own_source, own)], sems)
        place(mat, 0, assembled(mine, 1, False))
        place(mat, both, assembled(mate_resid, 0, False))
        sends = []
        for j, row in enumerate(copies):
            for copy in row:
                copy.wait()
            cols = pl.ds(j * CHUNK, CHUNK)
            fields = jnp.dot(mat[:, :both], near[:, cols], preferred_element_type=jnp.float32)
            fields = fields + jnp.dot(mat[:, both:], second[:, cols], preferred_element_type=jnp.float32)
            out[j] = fields
            send = pltpu.make_async_copy(out.at[j], early.at[:, cols], out_sems.at[j])
            send.start()
            sends.append(send)
            kernel_part[:, cols] = jnp.sum(own[:, cols].astype(jnp.float32) * fields, axis=0, keepdims=True)
        for send in sends:
            send.wait()

    @pl.when(par[0] == 0)
    def _():
        run(mate_near_source)

    @pl.when(par[0] == 1)
    def _():
        run(mate_source)


def late_kernel(inv_norm, par, scale, mine, far_resid, early_source, far_real, far_imag, mate_source, mate_near_source, adjoint, mat, far, second, early, out, sems, out_sems):
    both = early.shape[0]
    half = both // 2

    def run(second_source, second_resid):
        parts = [(far_real, far.at[:half]), (far_imag, far.at[half:]), (second_source, second), (early_source, early)]
        copies = fetches(parts, sems)
        place(mat, 0, assembled(far_resid, 1, True))
        place(mat, both, assembled(second_resid, 0, True))
        sends = []
        for j, row in enumerate(copies):
            for copy in row:
                copy.wait()
            cols = pl.ds(j * CHUNK, CHUNK)
            fields = early[:, cols] + jnp.dot(mat[:, :both], far[:, cols], preferred_element_type=jnp.float32)
            fields = fields + jnp.dot(mat[:, both:], second[:, cols], preferred_element_type=jnp.float32)
            out[j] = (fields * (inv_norm * scale[:, cols])).reshape(out.shape[1:])
            send = pltpu.make_async_copy(out.at[j], adjoint.at[:, :, cols], out_sems.at[j])
            send.start()
            sends.append(send)
        for send in sends:
            send.wait()

    @pl.when(par[0] == 0)
    def _():
        run(mate_source, mine)

    @pl.when(par[0] == 1)
    def _():
        run(mate_near_source, far_resid)


def ring_kernel(place_of, rows, above, below, out, slots):
    count = slots.shape[0]
    position = 0
    for piece, offset in ((below, -3), (rows, -1), (above, 2)):
        for i in range(piece.shape[0]):
            slots[lax.rem(place_of[0] + (offset + i + count), count)] = piece[i]
            position += 1
    assert position == count
    total = slots[0]
    for i in range(1, count):
        total = total + slots[i]
    out[...] = total


def ring_sum(place_of, rows, above, below, count):
    vmem = pl.BlockSpec(memory_space=pltpu.VMEM)
    return pl.pallas_call(
        ring_kernel,
        out_shape=jax.ShapeDtypeStruct(rows.shape[1:], jnp.float32),
        in_specs=[pl.BlockSpec(memory_space=pltpu.SMEM)] + [vmem] * 3,
        out_specs=vmem,
        scratch_shapes=[pltpu.VMEM((count,) + rows.shape[1:], jnp.float32)],
        cost_estimate=pl.CostEstimate(flops=0, bytes_accessed=1 << 17, transcendentals=0),
        compiler_params=pltpu.CompilerParams(vmem_limit_bytes=1 << 20),
        name="ring_sum",
    )(place_of, rows, above, below)


def early_fields(par, mine, mate_resid, own, mate, near, mate_near):
    both, cols = own.shape
    vmem = pl.BlockSpec(memory_space=pltpu.VMEM)
    anywhere = pl.BlockSpec(memory_space=pl.ANY)
    return pl.pallas_call(
        early_kernel,
        out_shape=(
            pltpu.HBM((both, cols), jnp.float32),
            jax.ShapeDtypeStruct((1, cols), jnp.float32),
        ),
        in_specs=[pl.BlockSpec(memory_space=pltpu.SMEM)] + [vmem] * 2 + [anywhere] * 4,
        out_specs=(pl.BlockSpec(memory_space=pltpu.HBM), vmem),
        scratch_shapes=[pltpu.VMEM((both, 2 * both), jnp.bfloat16)]
        + [pltpu.VMEM((both, cols), jnp.bfloat16)] * 3
        + [
            pltpu.VMEM((cols // CHUNK, both, CHUNK), jnp.float32),
            pltpu.SemaphoreType.DMA((3, cols // CHUNK)),
            pltpu.SemaphoreType.DMA((cols // CHUNK,)),
        ],
        cost_estimate=pl.CostEstimate(flops=4 * both * both * cols, bytes_accessed=10 * both * cols, transcendentals=0),
        compiler_params=pltpu.CompilerParams(vmem_limit_bytes=20 << 20),
        name="early",
    )(par, mine, mate_resid, own, mate, near, mate_near)


def late_fields(par, scale, mine, far_resid, far, early, mate, mate_near, inv_norm):
    both, cols = early.shape
    half = both // 2
    vmem = pl.BlockSpec(memory_space=pltpu.VMEM)
    hbm = pl.BlockSpec(memory_space=pltpu.HBM)

    def body(*refs):
        late_kernel(inv_norm, *refs)

    return pl.pallas_call(
        body,
        out_shape=jax.ShapeDtypeStruct((2, half, cols), jnp.float32),
        in_specs=[pl.BlockSpec(memory_space=pltpu.SMEM)] + [vmem] * 3 + [hbm] * 5,
        out_specs=hbm,
        scratch_shapes=[
            pltpu.VMEM((both, 2 * both), jnp.bfloat16),
            pltpu.VMEM((both, cols), jnp.bfloat16),
            pltpu.VMEM((both, cols), jnp.bfloat16),
            pltpu.VMEM((both, cols), jnp.float32),
            pltpu.VMEM((cols // CHUNK, 2, half, CHUNK), jnp.float32),
            pltpu.SemaphoreType.DMA((4, cols // CHUNK)),
            pltpu.SemaphoreType.DMA((cols // CHUNK,)),
        ],
        cost_estimate=pl.CostEstimate(flops=4 * both * both * cols, bytes_accessed=12 * both * cols, transcendentals=0),
        compiler_params=pltpu.CompilerParams(vmem_limit_bytes=62 << 20),
        name="late",
    )(par, scale, mine, far_resid, early, *far, mate, mate_near)


def shards(green, source_weight, observed, amp_weight, pair_used):
    row_count, col_count = green.shape[1:]
    block_count = lax.axis_size("cable")
    parts = lax.axis_size("grid")
    inv_norm = 1.0 / math.sqrt(col_count * parts)
    kernel_scale = inv_norm / (2.0 * math.sqrt(2.0 * block_count))
    parity = lax.axis_index("cable") % 2
    even = parity == 0
    par = parity.reshape(1)
    scale = source_weight[None, :]
    own = green.reshape(2 * row_count, col_count)
    pieces_count = parts // 2
    along_x = [list(range(i, parts, 2)) for i in range(2)]

    near = permuted(own, "cable", near_chip)
    mate = permuted(own, "cable", partner)

    slice_rows = row_count // pieces_count
    first = lax.axis_index("grid") // 2 * slice_rows
    packed = prepared(par, pair_used, first.reshape(1), observed, amp_weight, slice_rows)
    data_first = permuted(packed[0], "cable", partner)
    data_second = permuted(packed[1], "cable", near_chip)
    data = jnp.stack([data_first, jnp.where(even, data_second, packed[1])])

    lhs_first = (mate.astype(jnp.float32) * scale).astype(jnp.bfloat16)
    lhs_second = (own.astype(jnp.float32) * jnp.where(even, 1.0, scale)).astype(jnp.bfloat16)
    cuts = (green[0], green[1])
    near, lhs_first, lhs_second, cuts = lax.optimization_barrier((near, lhs_first, lhs_second, cuts))

    partials = correlations(par, scale, lhs_first, lhs_second, own, near, pieces_count)
    far = []
    for component in range(2):
        far.append(permuted(cuts[component], "cable", far_chip))
    mate_near = permuted(near, "cable", partner)
    pieces = lax.all_to_all(partials, "grid", 0, 0, tiled=True, axis_index_groups=along_x)
    total, wire = summed(pieces)
    other = permuted(wire, "grid", partner)
    resid = residuals(total, other, data, pieces_count, inv_norm)
    mine = lax.all_to_all(resid, "grid", 0, 0, tiled=True, axis_index_groups=along_x)
    mate_resid = permuted(mine[:, :1], "cable", partner)
    far_resid = permuted(mine, "cable", far_chip)
    early, kernel_part = early_fields(par, mine, mate_resid, own, mate, near, mate_near)
    kernel = kernel_part[0] * kernel_scale
    adjoint = late_fields(par, scale, mine, far_resid, far, early, mate, mate_near, inv_norm)
    distance = block_count // 2
    swapped = [permuted(kernel, "cable", lambda i: i ^ d) for d in (1, distance, distance + 1)]
    kernel = (kernel + swapped[0]) + (swapped[1] + swapped[2])

    def along_z(hops):
        return lambda i: i // distance * distance + (i + 2 * hops) % distance

    kernel = kernel.reshape(1, 16, -1)
    neighbours = [permuted(kernel, "cable", along_z(hops)) for hops in (-1, 1)]
    rows = jnp.concatenate([neighbours[0], kernel, neighbours[1]], axis=0)
    above = permuted(rows, "cable", along_z(3))
    below = permuted(rows[1:], "cable", along_z(-3))
    place_of = lax.axis_index("cable") % distance // 2
    kernel = ring_sum(place_of.reshape(1), rows, above, below, distance // 2).reshape(col_count)
    return (adjoint, kernel)


def solution(mesh):
    in_specs = (
        P(None, "cable", "grid"),
        P("grid"),
        P(None, None, "cable", None),
        P(None, "cable", None),
        P("cable", None),
    )
    out_specs = (P(None, "cable", "grid"), P("grid"))

    return jax.shard_map(shards, mesh=mesh, in_specs=in_specs, out_specs=out_specs, check_vma=False)
```

```python
import math

import jax
import jax.numpy as jnp
from jax import lax
from jax.experimental import pallas as pl
from jax.experimental.pallas import tpu as pltpu
from jax.sharding import PartitionSpec as P


CHUNK = 512
CORR_CHUNK = 1024
WIRE = jnp.bfloat16


def permuted(block, axis, source_of):
    size = lax.axis_size(axis)
    return lax.ppermute(block, axis, [(source_of(i) % size, i) for i in range(size)])


def partner(i):
    return i ^ 1


def near_chip(i):
    return i + 2 if i % 2 == 0 else i - 2


def far_chip(i):
    return i - 2 if i % 2 == 0 else i + 2


def whole(array):
    return pl.BlockSpec(array.shape, lambda j: (0,) * array.ndim)


def prep_kernel(par, used, first, observed, amp_weight, natural, second, square):
    rows = natural.shape[1]
    at = pl.ds(pl.multiple_of(first[0], rows), rows)
    masks = [used[0, o].astype(jnp.float32) for o in range(2)]
    natural[:2] = observed[0, :, at, :]
    natural[2] = amp_weight[0, at, :] * masks[0]

    @pl.when(par[0] == 0)
    def _():
        square[0] = observed[1, 0].T
        square[1] = -observed[1, 1].T
        square[2] = amp_weight[1].T * masks[1]
        second[...] = square[:, at, :]

    @pl.when(par[0] == 1)
    def _():
        second[:2] = observed[1, :, at, :]
        second[2] = amp_weight[1, at, :] * masks[1]


def prepared(par, used, first, observed, amp_weight, slice_rows):
    cols = amp_weight.shape[2]
    packed = (3, slice_rows, cols)
    smem = pl.BlockSpec(memory_space=pltpu.SMEM)
    return pl.pallas_call(
        prep_kernel,
        out_shape=(jax.ShapeDtypeStruct(packed, jnp.float32),) * 2,
        grid=(1,),
        in_specs=[smem, smem, smem, whole(observed), whole(amp_weight)],
        out_specs=(pl.BlockSpec(packed, lambda j: (0, 0, 0)),) * 2,
        scratch_shapes=[pltpu.VMEM((3, cols, cols), jnp.float32)],
        cost_estimate=pl.CostEstimate(flops=0, bytes_accessed=8 << 20, transcendentals=0),
        compiler_params=pltpu.CompilerParams(vmem_limit_bytes=8 << 20),
        name="prep",
    )(par, used, first, observed, amp_weight)


def sum_kernel(pieces, total, wire):
    value = pieces[0].astype(jnp.float32)
    for part in range(1, pieces.shape[0]):
        value = value + pieces[part].astype(jnp.float32)
    total[...] = value
    wire[...] = value.astype(wire.dtype)


def summed(pieces):
    vmem = pl.BlockSpec(memory_space=pltpu.VMEM)
    shape = pieces.shape[1:]
    return pl.pallas_call(
        sum_kernel,
        out_shape=(jax.ShapeDtypeStruct(shape, jnp.float32), jax.ShapeDtypeStruct(shape, WIRE)),
        in_specs=[vmem],
        out_specs=(vmem, vmem),
        cost_estimate=pl.CostEstimate(flops=0, bytes_accessed=1 << 20, transcendentals=0),
        compiler_params=pltpu.CompilerParams(vmem_limit_bytes=4 << 20),
        name="summed",
    )(pieces)


def resid_kernel(inv_norm, total, other, data, out):
    corr = inv_norm * (total[...] + other[...].astype(jnp.float32))
    resid = (data[:, 2:] * (corr - data[:, :2])).astype(jnp.bfloat16)
    for part in range(out.shape[0]):
        out[part] = resid


def residuals(total, other, data, parts, inv_norm):
    def body(*refs):
        resid_kernel(inv_norm, *refs)

    vmem = pl.BlockSpec(memory_space=pltpu.VMEM)
    return pl.pallas_call(
        body,
        out_shape=jax.ShapeDtypeStruct((parts,) + total.shape, jnp.bfloat16),
        in_specs=[vmem] * 3,
        out_specs=vmem,
        cost_estimate=pl.CostEstimate(flops=0, bytes_accessed=2 << 20, transcendentals=0),
        compiler_params=pltpu.CompilerParams(vmem_limit_bytes=6 << 20),
        name="resid",
    )(total, other, data)


def fetches(pairs, sems, chunk):
    copies = []
    for j in range(pairs[0][1].shape[1] // chunk):
        cols = pl.ds(j * chunk, chunk)
        row = []
        for i, (source, target) in enumerate(pairs):
            copy = pltpu.make_async_copy(source.at[:, cols], target.at[:, cols], sems.at[i, j])
            copy.start()
            row.append(copy)
        copies.append(row)
    return copies


def corr_kernel(par, scale, lhs_first, lhs_second, own, near_source, out, acc, near, sems):
    even = par[0] == 0
    for j, copies in enumerate(fetches([(near_source, near)], sems, CORR_CHUNK)):
        for copy in copies:
            copy.wait()
        cols = pl.ds(j * CORR_CHUNK, CORR_CHUNK)
        near_cols = near[:, cols]
        rhs_first = jnp.where(even, own[:, cols], near_cols)
        near_scale = jnp.where(even, scale[:, cols], 1.0)
        rhs_second = (near_cols.astype(jnp.float32) * near_scale).astype(jnp.bfloat16)
        for pair, (lhs, rhs) in enumerate(((lhs_first, rhs_first), (lhs_second, rhs_second))):
            products = lax.dot_general(
                lhs[:, cols], rhs, (((1,), (1,)), ((), ())), preferred_element_type=jnp.float32
            )
            if j == 0:
                acc[pair] = products
            else:
                acc[pair] += products

    parts, _, _, rows, cols = out.shape
    half = parts * rows
    for pair in range(2):
        real = acc[pair, :half, :cols] + acc[pair, half:, cols:]
        imag = acc[pair, :half, cols:] - acc[pair, half:, :cols]
        out[:, pair, 0] = real.reshape(parts, rows, cols).astype(out.dtype)
        out[:, pair, 1] = imag.reshape(parts, rows, cols).astype(out.dtype)


def correlations(par, scale, lhs_first, lhs_second, own, near, parts):
    both, cols = own.shape
    half = both // 2
    vmem = pl.BlockSpec(memory_space=pltpu.VMEM)
    return pl.pallas_call(
        corr_kernel,
        out_shape=jax.ShapeDtypeStruct((parts, 2, 2, half // parts, half), WIRE),
        in_specs=[pl.BlockSpec(memory_space=pltpu.SMEM)] + [vmem] * 4 + [pl.BlockSpec(memory_space=pl.ANY)],
        out_specs=vmem,
        scratch_shapes=[
            pltpu.VMEM((2, both, both), jnp.float32),
            pltpu.VMEM((both, cols), jnp.bfloat16),
            pltpu.SemaphoreType.DMA((1, cols // CORR_CHUNK)),
        ],
        cost_estimate=pl.CostEstimate(flops=4 * both * both * cols, bytes_accessed=8 * both * cols, transcendentals=0),
        compiler_params=pltpu.CompilerParams(vmem_limit_bytes=24 << 20),
        name="corr",
    )(par, scale, lhs_first, lhs_second, own, near)


def assembled(gathered, pair, turned):
    real, imag = (gathered[:, pair, c].reshape(-1, gathered.shape[-1]) for c in range(2))
    if turned:
        real = real.astype(jnp.float32).T.astype(jnp.bfloat16)
        imag = (-imag.astype(jnp.float32)).T.astype(jnp.bfloat16)
    return real, imag


def place(mat, base, block):
    real, imag = block
    half = real.shape[0]
    mat[:half, base : base + half] = real
    mat[half:, base + half : base + 2 * half] = real
    mat[:half, base + half : base + 2 * half] = imag
    mat[half:, base : base + half] = -imag


def early_kernel(par, mine, mate_resid, own_source, mate_source, near_source, mate_near_source, early, kernel_part, mat, own, blocks, out, sems, out_sems):
    both = own.shape[0]

    def run(second_source):
        parts = [(near_source, blocks.at[:both]), (second_source, blocks.at[both:]), (own_source, own)]
        copies = fetches(parts, sems, CHUNK)
        place(mat, 0, assembled(mine, 1, False))
        place(mat, both, assembled(mate_resid, 0, False))
        sends = []
        for j, row in enumerate(copies):
            for copy in row:
                copy.wait()
            cols = pl.ds(j * CHUNK, CHUNK)
            fields = jnp.dot(mat[...], blocks[:, cols], preferred_element_type=jnp.float32)
            out[j] = fields
            send = pltpu.make_async_copy(out.at[j], early.at[:, cols], out_sems.at[j])
            send.start()
            sends.append(send)
            kernel_part[:, cols] = jnp.sum(own[:, cols].astype(jnp.float32) * fields, axis=0, keepdims=True)
        for send in sends:
            send.wait()

    @pl.when(par[0] == 0)
    def _():
        run(mate_near_source)

    @pl.when(par[0] == 1)
    def _():
        run(mate_source)


def turn_kernel(par, mine, far_resid, mat):
    both = mat.shape[0]
    place(mat, 0, assembled(far_resid, 1, True))

    @pl.when(par[0] == 0)
    def _():
        place(mat, both, assembled(mine, 0, True))

    @pl.when(par[0] == 1)
    def _():
        place(mat, both, assembled(far_resid, 0, True))


def late_kernel(inv_norm, par, scale, mat, early_source, far_real, far_imag, mate_source, mate_near_source, adjoint, blocks, early, out, sems, out_sems):
    both = early.shape[0]
    half = both // 2

    def run(second_source):
        parts = [
            (far_real, blocks.at[:half]),
            (far_imag, blocks.at[half:both]),
            (second_source, blocks.at[both:]),
            (early_source, early),
        ]
        copies = fetches(parts, sems, CHUNK)
        sends = []
        for j, row in enumerate(copies):
            for copy in row:
                copy.wait()
            cols = pl.ds(j * CHUNK, CHUNK)
            fields = early[:, cols] + jnp.dot(mat[...], blocks[:, cols], preferred_element_type=jnp.float32)
            out[j] = (fields * (inv_norm * scale[:, cols])).reshape(out.shape[1:])
            send = pltpu.make_async_copy(out.at[j], adjoint.at[:, :, cols], out_sems.at[j])
            send.start()
            sends.append(send)
        for send in sends:
            send.wait()

    @pl.when(par[0] == 0)
    def _():
        run(mate_source)

    @pl.when(par[0] == 1)
    def _():
        run(mate_near_source)


def ring_kernel(place_of, rows, above, below, out, slots):
    count = slots.shape[0]
    position = 0
    for piece, offset in ((below, -3), (rows, -1), (above, 2)):
        for i in range(piece.shape[0]):
            slots[lax.rem(place_of[0] + (offset + i + count), count)] = piece[i]
            position += 1
    assert position == count
    total = slots[0]
    for i in range(1, count):
        total = total + slots[i]
    out[...] = total


def ring_sum(place_of, rows, above, below, count):
    vmem = pl.BlockSpec(memory_space=pltpu.VMEM)
    return pl.pallas_call(
        ring_kernel,
        out_shape=jax.ShapeDtypeStruct(rows.shape[1:], jnp.float32),
        in_specs=[pl.BlockSpec(memory_space=pltpu.SMEM)] + [vmem] * 3,
        out_specs=vmem,
        scratch_shapes=[pltpu.VMEM((count,) + rows.shape[1:], jnp.float32)],
        cost_estimate=pl.CostEstimate(flops=0, bytes_accessed=1 << 17, transcendentals=0),
        compiler_params=pltpu.CompilerParams(vmem_limit_bytes=1 << 20),
        name="ring_sum",
    )(place_of, rows, above, below)


def early_fields(par, mine, mate_resid, own, mate, near, mate_near):
    both, cols = own.shape
    vmem = pl.BlockSpec(memory_space=pltpu.VMEM)
    anywhere = pl.BlockSpec(memory_space=pl.ANY)
    return pl.pallas_call(
        early_kernel,
        out_shape=(
            pltpu.HBM((both, cols), jnp.float32),
            jax.ShapeDtypeStruct((1, cols), jnp.float32),
        ),
        in_specs=[pl.BlockSpec(memory_space=pltpu.SMEM)] + [vmem] * 2 + [anywhere] * 4,
        out_specs=(pl.BlockSpec(memory_space=pltpu.HBM), vmem),
        scratch_shapes=[pltpu.VMEM((both, 2 * both), jnp.bfloat16)]
        + [
            pltpu.VMEM((both, cols), jnp.bfloat16),
            pltpu.VMEM((2 * both, cols), jnp.bfloat16),
            pltpu.VMEM((cols // CHUNK, both, CHUNK), jnp.float32),
            pltpu.SemaphoreType.DMA((3, cols // CHUNK)),
            pltpu.SemaphoreType.DMA((cols // CHUNK,)),
        ],
        cost_estimate=pl.CostEstimate(flops=4 * both * both * cols, bytes_accessed=10 * both * cols, transcendentals=0),
        compiler_params=pltpu.CompilerParams(vmem_limit_bytes=20 << 20),
        name="early",
    )(par, mine, mate_resid, own, mate, near, mate_near)


def turned(par, mine, far_resid, both):
    vmem = pl.BlockSpec(memory_space=pltpu.VMEM)
    return pl.pallas_call(
        turn_kernel,
        out_shape=jax.ShapeDtypeStruct((both, 2 * both), jnp.bfloat16),
        in_specs=[pl.BlockSpec(memory_space=pltpu.SMEM), vmem, vmem],
        out_specs=vmem,
        cost_estimate=pl.CostEstimate(flops=0, bytes_accessed=2 << 20, transcendentals=0),
        compiler_params=pltpu.CompilerParams(vmem_limit_bytes=8 << 20),
        name="turned",
    )(par, mine, far_resid)


def late_fields(par, scale, mat, far, early, mate, mate_near, inv_norm):
    both, cols = early.shape
    half = both // 2
    vmem = pl.BlockSpec(memory_space=pltpu.VMEM)
    hbm = pl.BlockSpec(memory_space=pltpu.HBM)

    def body(*refs):
        late_kernel(inv_norm, *refs)

    return pl.pallas_call(
        body,
        out_shape=jax.ShapeDtypeStruct((2, half, cols), jnp.float32),
        in_specs=[pl.BlockSpec(memory_space=pltpu.SMEM)] + [vmem] * 2 + [hbm] * 5,
        out_specs=hbm,
        scratch_shapes=[
            pltpu.VMEM((2 * both, cols), jnp.bfloat16),
            pltpu.VMEM((both, cols), jnp.float32),
            pltpu.VMEM((cols // CHUNK, 2, half, CHUNK), jnp.float32),
            pltpu.SemaphoreType.DMA((4, cols // CHUNK)),
            pltpu.SemaphoreType.DMA((cols // CHUNK,)),
        ],
        cost_estimate=pl.CostEstimate(flops=4 * both * both * cols, bytes_accessed=12 * both * cols, transcendentals=0),
        compiler_params=pltpu.CompilerParams(vmem_limit_bytes=48 << 20),
        name="late",
    )(par, scale, mat, early, *far, mate, mate_near)


def shards(green, source_weight, observed, amp_weight, pair_used):
    row_count, col_count = green.shape[1:]
    block_count = lax.axis_size("cable")
    parts = lax.axis_size("grid")
    inv_norm = 1.0 / math.sqrt(col_count * parts)
    kernel_scale = inv_norm / (2.0 * math.sqrt(2.0 * block_count))
    parity = lax.axis_index("cable") % 2
    even = parity == 0
    par = parity.reshape(1)
    scale = source_weight[None, :]
    own = green.reshape(2 * row_count, col_count)
    pieces_count = parts // 2
    along_x = [list(range(i, parts, 2)) for i in range(2)]

    near = permuted(own, "cable", near_chip)
    mate = permuted(own, "cable", partner)

    slice_rows = row_count // pieces_count
    first = lax.axis_index("grid") // 2 * slice_rows
    packed = prepared(par, pair_used, first.reshape(1), observed, amp_weight, slice_rows)
    data_first = permuted(packed[0], "cable", partner)
    data_second = permuted(packed[1], "cable", near_chip)
    data = jnp.stack([data_first, jnp.where(even, data_second, packed[1])])

    lhs_first = (mate.astype(jnp.float32) * scale).astype(jnp.bfloat16)
    lhs_second = (own.astype(jnp.float32) * jnp.where(even, 1.0, scale)).astype(jnp.bfloat16)
    cuts = (green[0], green[1])
    near, lhs_first, lhs_second, cuts = lax.optimization_barrier((near, lhs_first, lhs_second, cuts))

    partials = correlations(par, scale, lhs_first, lhs_second, own, near, pieces_count)
    far = []
    for component in range(2):
        far.append(permuted(cuts[component], "cable", far_chip))
    mate_near = permuted(near, "cable", partner)
    pieces = lax.all_to_all(partials, "grid", 0, 0, tiled=True, axis_index_groups=along_x)
    total, wire = summed(pieces)
    other = permuted(wire, "grid", partner)
    resid = residuals(total, other, data, pieces_count, inv_norm)
    mine = lax.all_to_all(resid, "grid", 0, 0, tiled=True, axis_index_groups=along_x)
    mate_resid = permuted(mine[:, :1], "cable", partner)
    far_resid = permuted(mine, "cable", far_chip)
    early, kernel_part = early_fields(par, mine, mate_resid, own, mate, near, mate_near)
    kernel = kernel_part[0] * kernel_scale
    mat = turned(par, mine, far_resid, 2 * row_count)
    adjoint = late_fields(par, scale, mat, far, early, mate, mate_near, inv_norm)
    distance = block_count // 2
    swapped = [permuted(kernel, "cable", lambda i: i ^ d) for d in (1, distance, distance + 1)]
    kernel = (kernel + swapped[0]) + (swapped[1] + swapped[2])

    def along_z(hops):
        return lambda i: i // distance * distance + (i + 2 * hops) % distance

    kernel = kernel.reshape(1, 16, -1)
    neighbours = [permuted(kernel, "cable", along_z(hops)) for hops in (-1, 1)]
    rows = jnp.concatenate([neighbours[0], kernel, neighbours[1]], axis=0)
    above = permuted(rows, "cable", along_z(3))
    below = permuted(rows[1:], "cable", along_z(-3))
    place_of = lax.axis_index("cable") % distance // 2
    kernel = ring_sum(place_of.reshape(1), rows, above, below, distance // 2).reshape(col_count)
    return (adjoint, kernel)


def solution(mesh):
    in_specs = (
        P(None, "cable", "grid"),
        P("grid"),
        P(None, None, "cable", None),
        P(None, "cable", None),
        P("cable", None),
    )
    out_specs = (P(None, "cable", "grid"), P("grid"))

    return jax.shard_map(shards, mesh=mesh, in_specs=in_specs, out_specs=out_specs, check_vma=False)
```

```python
import math

import jax
import jax.numpy as jnp
from jax import lax
from jax.experimental import pallas as pl
from jax.experimental.pallas import tpu as pltpu
from jax.sharding import PartitionSpec as P


CHUNK = 512
CORR_CHUNK = 1024
WIRE = jnp.bfloat16


def permuted(block, axis, source_of):
    size = lax.axis_size(axis)
    return lax.ppermute(block, axis, [(source_of(i) % size, i) for i in range(size)])


def partner(i):
    return i ^ 1


def near_chip(i):
    return i + 2 if i % 2 == 0 else i - 2


def far_chip(i):
    return i - 2 if i % 2 == 0 else i + 2


def whole(array):
    return pl.BlockSpec(array.shape, lambda j: (0,) * array.ndim)


def prep_kernel(par, used, first, observed, amp_weight, natural, second, square):
    rows = natural.shape[1]
    at = pl.ds(pl.multiple_of(first[0], rows), rows)
    masks = [used[0, o].astype(jnp.float32) for o in range(2)]
    natural[:2] = observed[0, :, at, :]
    natural[2] = amp_weight[0, at, :] * masks[0]

    @pl.when(par[0] == 0)
    def _():
        square[0] = observed[1, 0].T
        square[1] = -observed[1, 1].T
        square[2] = amp_weight[1].T * masks[1]
        second[...] = square[:, at, :]

    @pl.when(par[0] == 1)
    def _():
        second[:2] = observed[1, :, at, :]
        second[2] = amp_weight[1, at, :] * masks[1]


def prepared(par, used, first, observed, amp_weight, slice_rows):
    cols = amp_weight.shape[2]
    packed = (3, slice_rows, cols)
    smem = pl.BlockSpec(memory_space=pltpu.SMEM)
    return pl.pallas_call(
        prep_kernel,
        out_shape=(jax.ShapeDtypeStruct(packed, jnp.float32),) * 2,
        grid=(1,),
        in_specs=[smem, smem, smem, whole(observed), whole(amp_weight)],
        out_specs=(pl.BlockSpec(packed, lambda j: (0, 0, 0)),) * 2,
        scratch_shapes=[pltpu.VMEM((3, cols, cols), jnp.float32)],
        cost_estimate=pl.CostEstimate(flops=0, bytes_accessed=8 << 20, transcendentals=0),
        compiler_params=pltpu.CompilerParams(vmem_limit_bytes=8 << 20),
        name="prep",
    )(par, used, first, observed, amp_weight)


def sum_kernel(pieces, total, wire):
    value = pieces[0].astype(jnp.float32)
    for part in range(1, pieces.shape[0]):
        value = value + pieces[part].astype(jnp.float32)
    total[...] = value
    wire[...] = value.astype(wire.dtype)


def summed(pieces):
    vmem = pl.BlockSpec(memory_space=pltpu.VMEM)
    shape = pieces.shape[1:]
    return pl.pallas_call(
        sum_kernel,
        out_shape=(jax.ShapeDtypeStruct(shape, jnp.float32), jax.ShapeDtypeStruct(shape, WIRE)),
        in_specs=[vmem],
        out_specs=(vmem, vmem),
        cost_estimate=pl.CostEstimate(flops=0, bytes_accessed=1 << 20, transcendentals=0),
        compiler_params=pltpu.CompilerParams(vmem_limit_bytes=4 << 20),
        name="summed",
    )(pieces)


def resid_kernel(inv_norm, total, other, data, out):
    corr = inv_norm * (total[...] + other[...].astype(jnp.float32))
    resid = (data[:, 2:] * (corr - data[:, :2])).astype(jnp.bfloat16)
    for part in range(out.shape[0]):
        out[part] = resid


def residuals(total, other, data, parts, inv_norm):
    def body(*refs):
        resid_kernel(inv_norm, *refs)

    vmem = pl.BlockSpec(memory_space=pltpu.VMEM)
    return pl.pallas_call(
        body,
        out_shape=jax.ShapeDtypeStruct((parts,) + total.shape, jnp.bfloat16),
        in_specs=[vmem] * 3,
        out_specs=vmem,
        cost_estimate=pl.CostEstimate(flops=0, bytes_accessed=2 << 20, transcendentals=0),
        compiler_params=pltpu.CompilerParams(vmem_limit_bytes=6 << 20),
        name="resid",
    )(total, other, data)


def fetches(pairs, sems, chunk, begin=0):
    copies = []
    for j in range(pairs[0][1].shape[1] // chunk):
        row = []
        for i, (source, target) in enumerate(pairs):
            copy = pltpu.make_async_copy(
                source.at[:, pl.ds(begin + j * chunk, chunk)], target.at[:, pl.ds(j * chunk, chunk)], sems.at[i, j]
            )
            copy.start()
            row.append(copy)
        copies.append(row)
    return copies


def corr_kernel(par, scale, lhs_first, lhs_second, own, near_source, out, acc, near, sems):
    even = par[0] == 0
    for j, copies in enumerate(fetches([(near_source, near)], sems, CORR_CHUNK)):
        for copy in copies:
            copy.wait()
        cols = pl.ds(j * CORR_CHUNK, CORR_CHUNK)
        near_cols = near[:, cols]
        rhs_first = jnp.where(even, own[:, cols], near_cols)
        near_scale = jnp.where(even, scale[:, cols], 1.0)
        rhs_second = (near_cols.astype(jnp.float32) * near_scale).astype(jnp.bfloat16)
        for pair, (lhs, rhs) in enumerate(((lhs_first, rhs_first), (lhs_second, rhs_second))):
            products = lax.dot_general(
                lhs[:, cols], rhs, (((1,), (1,)), ((), ())), preferred_element_type=jnp.float32
            )
            if j == 0:
                acc[pair] = products
            else:
                acc[pair] += products

    parts, _, _, rows, cols = out.shape
    half = parts * rows
    for pair in range(2):
        real = acc[pair, :half, :cols] + acc[pair, half:, cols:]
        imag = acc[pair, :half, cols:] - acc[pair, half:, :cols]
        out[:, pair, 0] = real.reshape(parts, rows, cols).astype(out.dtype)
        out[:, pair, 1] = imag.reshape(parts, rows, cols).astype(out.dtype)


def correlations(par, scale, lhs_first, lhs_second, own, near, parts):
    both, cols = own.shape
    half = both // 2
    vmem = pl.BlockSpec(memory_space=pltpu.VMEM)
    return pl.pallas_call(
        corr_kernel,
        out_shape=jax.ShapeDtypeStruct((parts, 2, 2, half // parts, half), WIRE),
        in_specs=[pl.BlockSpec(memory_space=pltpu.SMEM)] + [vmem] * 4 + [pl.BlockSpec(memory_space=pl.ANY)],
        out_specs=vmem,
        scratch_shapes=[
            pltpu.VMEM((2, both, both), jnp.float32),
            pltpu.VMEM((both, cols), jnp.bfloat16),
            pltpu.SemaphoreType.DMA((1, cols // CORR_CHUNK)),
        ],
        cost_estimate=pl.CostEstimate(flops=4 * both * both * cols, bytes_accessed=8 * both * cols, transcendentals=0),
        compiler_params=pltpu.CompilerParams(vmem_limit_bytes=24 << 20),
        name="corr",
    )(par, scale, lhs_first, lhs_second, own, near)


def assembled(gathered, pair, turned):
    real, imag = (gathered[:, pair, c].reshape(-1, gathered.shape[-1]) for c in range(2))
    if turned:
        real = real.astype(jnp.float32).T.astype(jnp.bfloat16)
        imag = (-imag.astype(jnp.float32)).T.astype(jnp.bfloat16)
    return real, imag


def place(mat, base, block):
    real, imag = block
    half = real.shape[0]
    mat[:half, base : base + half] = real
    mat[half:, base + half : base + 2 * half] = real
    mat[:half, base + half : base + 2 * half] = imag
    mat[half:, base : base + half] = -imag


def early_kernel(par, mine, mate_resid, own_source, mate_source, near_source, mate_near_source, early, kernel_part, mat, own, blocks, out, sems, out_sems):
    both = own.shape[0]

    def run(second_source):
        parts = [(near_source, blocks.at[:both]), (second_source, blocks.at[both:]), (own_source, own)]
        copies = fetches(parts, sems, CHUNK)
        place(mat, 0, assembled(mine, 1, False))
        place(mat, both, assembled(mate_resid, 0, False))
        sends = []
        for j, row in enumerate(copies):
            for copy in row:
                copy.wait()
            cols = pl.ds(j * CHUNK, CHUNK)
            fields = jnp.dot(mat[...], blocks[:, cols], preferred_element_type=jnp.float32)
            out[j] = fields
            send = pltpu.make_async_copy(out.at[j], early.at[:, cols], out_sems.at[j])
            send.start()
            sends.append(send)
            kernel_part[:, cols] = jnp.sum(own[:, cols].astype(jnp.float32) * fields, axis=0, keepdims=True)
        for send in sends:
            send.wait()

    @pl.when(par[0] == 0)
    def _():
        run(mate_near_source)

    @pl.when(par[0] == 1)
    def _():
        run(mate_source)


def turn_kernel(par, mine, far_resid, mat):
    both = mat.shape[0]
    place(mat, 0, assembled(far_resid, 1, True))

    @pl.when(par[0] == 0)
    def _():
        place(mat, both, assembled(mine, 0, True))

    @pl.when(par[0] == 1)
    def _():
        place(mat, both, assembled(far_resid, 0, True))


def late_kernel(inv_norm, begin, par, scale, mat_source, early_source, far_real, far_imag, mate_source, mate_near_source, *refs):
    adjoint, mat, blocks, early, out, mat_sem, sems, out_sems = refs[-8:]
    both = early.shape[0]
    half = both // 2

    def run(second_source):
        parts = [
            (far_real, blocks.at[:half]),
            (far_imag, blocks.at[half:both]),
            (second_source, blocks.at[both:]),
            (early_source, early),
        ]
        mat_copy = pltpu.make_async_copy(mat_source, mat, mat_sem)
        mat_copy.start()
        copies = fetches(parts, sems, CHUNK, begin)
        mat_copy.wait()
        sends = []
        for j, row in enumerate(copies):
            for copy in row:
                copy.wait()
            cols = pl.ds(j * CHUNK, CHUNK)
            target = pl.ds(begin + j * CHUNK, CHUNK)
            fields = early[:, cols] + jnp.dot(mat[...], blocks[:, cols], preferred_element_type=jnp.float32)
            out[j] = (fields * (inv_norm * scale[:, target])).reshape(out.shape[1:])
            send = pltpu.make_async_copy(out.at[j], adjoint.at[:, :, target], out_sems.at[j])
            send.start()
            sends.append(send)
        for send in sends:
            send.wait()

    @pl.when(par[0] == 0)
    def _():
        run(mate_source)

    @pl.when(par[0] == 1)
    def _():
        run(mate_near_source)


def ring_kernel(place_of, rows, above, below, out, slots):
    count = slots.shape[0]
    position = 0
    for piece, offset in ((below, -3), (rows, -1), (above, 2)):
        for i in range(piece.shape[0]):
            slots[lax.rem(place_of[0] + (offset + i + count), count)] = piece[i]
            position += 1
    assert position == count
    total = slots[0]
    for i in range(1, count):
        total = total + slots[i]
    out[...] = total


def ring_sum(place_of, rows, above, below, count):
    vmem = pl.BlockSpec(memory_space=pltpu.VMEM)
    return pl.pallas_call(
        ring_kernel,
        out_shape=jax.ShapeDtypeStruct(rows.shape[1:], jnp.float32),
        in_specs=[pl.BlockSpec(memory_space=pltpu.SMEM)] + [vmem] * 3,
        out_specs=vmem,
        scratch_shapes=[pltpu.VMEM((count,) + rows.shape[1:], jnp.float32)],
        cost_estimate=pl.CostEstimate(flops=0, bytes_accessed=1 << 17, transcendentals=0),
        compiler_params=pltpu.CompilerParams(vmem_limit_bytes=1 << 20),
        name="ring_sum",
    )(place_of, rows, above, below)


def early_fields(par, mine, mate_resid, own, mate, near, mate_near):
    both, cols = own.shape
    vmem = pl.BlockSpec(memory_space=pltpu.VMEM)
    anywhere = pl.BlockSpec(memory_space=pl.ANY)
    return pl.pallas_call(
        early_kernel,
        out_shape=(
            pltpu.HBM((both, cols), jnp.float32),
            jax.ShapeDtypeStruct((1, cols), jnp.float32),
        ),
        in_specs=[pl.BlockSpec(memory_space=pltpu.SMEM)] + [vmem] * 2 + [anywhere] * 4,
        out_specs=(pl.BlockSpec(memory_space=pltpu.HBM), vmem),
        scratch_shapes=[pltpu.VMEM((both, 2 * both), jnp.bfloat16)]
        + [
            pltpu.VMEM((both, cols), jnp.bfloat16),
            pltpu.VMEM((2 * both, cols), jnp.bfloat16),
            pltpu.VMEM((cols // CHUNK, both, CHUNK), jnp.float32),
            pltpu.SemaphoreType.DMA((3, cols // CHUNK)),
            pltpu.SemaphoreType.DMA((cols // CHUNK,)),
        ],
        cost_estimate=pl.CostEstimate(flops=4 * both * both * cols, bytes_accessed=10 * both * cols, transcendentals=0),
        compiler_params=pltpu.CompilerParams(vmem_limit_bytes=20 << 20),
        name="early",
    )(par, mine, mate_resid, own, mate, near, mate_near)


def turned(par, mine, far_resid, both):
    vmem = pl.BlockSpec(memory_space=pltpu.VMEM)
    return pl.pallas_call(
        turn_kernel,
        out_shape=pltpu.HBM((both, 2 * both), jnp.bfloat16),
        in_specs=[pl.BlockSpec(memory_space=pltpu.SMEM), vmem, vmem],
        out_specs=pl.BlockSpec((both, 2 * both), lambda: (0, 0)),
        cost_estimate=pl.CostEstimate(flops=0, bytes_accessed=2 << 20, transcendentals=0),
        compiler_params=pltpu.CompilerParams(vmem_limit_bytes=8 << 20),
        name="turned",
    )(par, mine, far_resid)


def late_fields(par, scale, mat, far, early, mate, mate_near, inv_norm, begin, count, partial=None):
    both, cols = early.shape
    half = both // 2
    vmem = pl.BlockSpec(memory_space=pltpu.VMEM)
    hbm = pl.BlockSpec(memory_space=pltpu.HBM)
    before = () if partial is None else (partial,)

    def body(*refs):
        late_kernel(inv_norm, begin, *refs)

    return pl.pallas_call(
        body,
        out_shape=jax.ShapeDtypeStruct((2, half, cols), jnp.float32),
        in_specs=[pl.BlockSpec(memory_space=pltpu.SMEM), vmem] + [hbm] * (6 + len(before)),
        out_specs=hbm,
        scratch_shapes=[
            pltpu.VMEM((both, 2 * both), jnp.bfloat16),
            pltpu.VMEM((2 * both, count), jnp.bfloat16),
            pltpu.VMEM((both, count), jnp.float32),
            pltpu.VMEM((count // CHUNK, 2, half, CHUNK), jnp.float32),
            pltpu.SemaphoreType.DMA,
            pltpu.SemaphoreType.DMA((4, count // CHUNK)),
            pltpu.SemaphoreType.DMA((count // CHUNK,)),
        ],
        input_output_aliases={8: 0} if before else {},
        cost_estimate=pl.CostEstimate(
            flops=4 * both * both * count, bytes_accessed=12 * both * count, transcendentals=0
        ),
        compiler_params=pltpu.CompilerParams(vmem_limit_bytes=62 << 20),
        name="late",
    )(par, scale, mat, early, *far, mate, mate_near, *before)


def shards(green, source_weight, observed, amp_weight, pair_used):
    row_count, col_count = green.shape[1:]
    block_count = lax.axis_size("cable")
    parts = lax.axis_size("grid")
    inv_norm = 1.0 / math.sqrt(col_count * parts)
    kernel_scale = inv_norm / (2.0 * math.sqrt(2.0 * block_count))
    parity = lax.axis_index("cable") % 2
    even = parity == 0
    par = parity.reshape(1)
    scale = source_weight[None, :]
    own = green.reshape(2 * row_count, col_count)
    pieces_count = parts // 2
    along_x = [list(range(i, parts, 2)) for i in range(2)]

    near = permuted(own, "cable", near_chip)
    mate = permuted(own, "cable", partner)

    slice_rows = row_count // pieces_count
    first = lax.axis_index("grid") // 2 * slice_rows
    packed = prepared(par, pair_used, first.reshape(1), observed, amp_weight, slice_rows)
    data_first = permuted(packed[0], "cable", partner)
    data_second = permuted(packed[1], "cable", near_chip)
    data = jnp.stack([data_first, jnp.where(even, data_second, packed[1])])

    lhs_first = (mate.astype(jnp.float32) * scale).astype(jnp.bfloat16)
    lhs_second = (own.astype(jnp.float32) * jnp.where(even, 1.0, scale)).astype(jnp.bfloat16)
    cuts = (green[0], green[1])
    near, lhs_first, lhs_second, cuts = lax.optimization_barrier((near, lhs_first, lhs_second, cuts))

    partials = correlations(par, scale, lhs_first, lhs_second, own, near, pieces_count)
    far = []
    for component in range(2):
        far.append(permuted(cuts[component], "cable", far_chip))
    mate_near = permuted(near, "cable", partner)
    pieces = lax.all_to_all(partials, "grid", 0, 0, tiled=True, axis_index_groups=along_x)
    total, wire = summed(pieces)
    other = permuted(wire, "grid", partner)
    resid = residuals(total, other, data, pieces_count, inv_norm)
    mine = lax.all_to_all(resid, "grid", 0, 0, tiled=True, axis_index_groups=along_x)
    mate_resid = permuted(mine[:, :1], "cable", partner)
    far_resid = permuted(mine, "cable", far_chip)
    early, kernel_part = early_fields(par, mine, mate_resid, own, mate, near, mate_near)
    kernel = kernel_part[0] * kernel_scale
    mat = turned(par, mine, far_resid, 2 * row_count)
    adjoint = None
    for part in range(2):
        count = col_count // 2
        adjoint = late_fields(
            par, scale, mat, far, early, mate, mate_near, inv_norm, part * count, count, adjoint
        )
    distance = block_count // 2
    swapped = [permuted(kernel, "cable", lambda i: i ^ d) for d in (1, distance, distance + 1)]
    kernel = (kernel + swapped[0]) + (swapped[1] + swapped[2])

    def along_z(hops):
        return lambda i: i // distance * distance + (i + 2 * hops) % distance

    kernel = kernel.reshape(1, 16, -1)
    neighbours = [permuted(kernel, "cable", along_z(hops)) for hops in (-1, 1)]
    rows = jnp.concatenate([neighbours[0], kernel, neighbours[1]], axis=0)
    above = permuted(rows, "cable", along_z(3))
    below = permuted(rows[1:], "cable", along_z(-3))
    place_of = lax.axis_index("cable") % distance // 2
    kernel = ring_sum(place_of.reshape(1), rows, above, below, distance // 2).reshape(col_count)
    return (adjoint, kernel)


def solution(mesh):
    in_specs = (
        P(None, "cable", "grid"),
        P("grid"),
        P(None, None, "cable", None),
        P(None, "cable", None),
        P("cable", None),
    )
    out_specs = (P(None, "cable", "grid"), P("grid"))

    return jax.shard_map(shards, mesh=mesh, in_specs=in_specs, out_specs=out_specs, check_vma=False)
```

```python
import math

import jax
import jax.numpy as jnp
from jax import lax
from jax.experimental import pallas as pl
from jax.experimental.pallas import tpu as pltpu
from jax.sharding import PartitionSpec as P


CHUNK = 512
CORR_CHUNK = 1024
WIRE = jnp.bfloat16


def permuted(block, axis, source_of):
    size = lax.axis_size(axis)
    return lax.ppermute(block, axis, [(source_of(i) % size, i) for i in range(size)])


def partner(i):
    return i ^ 1


def near_chip(i):
    return i + 2 if i % 2 == 0 else i - 2


def far_chip(i):
    return i - 2 if i % 2 == 0 else i + 2


def whole(array):
    return pl.BlockSpec(array.shape, lambda j: (0,) * array.ndim)


def prep_kernel(par, used, first, observed, amp_weight, natural, second, square):
    rows = natural.shape[1]
    at = pl.ds(pl.multiple_of(first[0], rows), rows)
    masks = [used[0, o].astype(jnp.float32) for o in range(2)]
    natural[:2] = observed[0, :, at, :]
    natural[2] = amp_weight[0, at, :] * masks[0]

    @pl.when(par[0] == 0)
    def _():
        square[0] = observed[1, 0].T
        square[1] = -observed[1, 1].T
        square[2] = amp_weight[1].T * masks[1]
        second[...] = square[:, at, :]

    @pl.when(par[0] == 1)
    def _():
        second[:2] = observed[1, :, at, :]
        second[2] = amp_weight[1, at, :] * masks[1]


def prepared(par, used, first, observed, amp_weight, slice_rows):
    cols = amp_weight.shape[2]
    packed = (3, slice_rows, cols)
    smem = pl.BlockSpec(memory_space=pltpu.SMEM)
    return pl.pallas_call(
        prep_kernel,
        out_shape=(jax.ShapeDtypeStruct(packed, jnp.float32),) * 2,
        grid=(1,),
        in_specs=[smem, smem, smem, whole(observed), whole(amp_weight)],
        out_specs=(pl.BlockSpec(packed, lambda j: (0, 0, 0)),) * 2,
        scratch_shapes=[pltpu.VMEM((3, cols, cols), jnp.float32)],
        cost_estimate=pl.CostEstimate(flops=0, bytes_accessed=8 << 20, transcendentals=0),
        compiler_params=pltpu.CompilerParams(vmem_limit_bytes=8 << 20),
        name="prep",
    )(par, used, first, observed, amp_weight)


def sum_kernel(pieces, total, wire):
    value = pieces[0].astype(jnp.float32)
    for part in range(1, pieces.shape[0]):
        value = value + pieces[part].astype(jnp.float32)
    total[...] = value
    wire[...] = value.astype(wire.dtype)


def summed(pieces):
    vmem = pl.BlockSpec(memory_space=pltpu.VMEM)
    shape = pieces.shape[1:]
    return pl.pallas_call(
        sum_kernel,
        out_shape=(jax.ShapeDtypeStruct(shape, jnp.float32), jax.ShapeDtypeStruct(shape, WIRE)),
        in_specs=[vmem],
        out_specs=(vmem, vmem),
        cost_estimate=pl.CostEstimate(flops=0, bytes_accessed=1 << 20, transcendentals=0),
        compiler_params=pltpu.CompilerParams(vmem_limit_bytes=4 << 20),
        name="summed",
    )(pieces)


def resid_kernel(inv_norm, total, other, data, out):
    corr = inv_norm * (total[...] + other[...].astype(jnp.float32))
    resid = (data[:, 2:] * (corr - data[:, :2])).astype(jnp.bfloat16)
    for part in range(out.shape[0]):
        out[part] = resid


def residuals(total, other, data, parts, inv_norm):
    def body(*refs):
        resid_kernel(inv_norm, *refs)

    vmem = pl.BlockSpec(memory_space=pltpu.VMEM)
    return pl.pallas_call(
        body,
        out_shape=jax.ShapeDtypeStruct((parts,) + total.shape, jnp.bfloat16),
        in_specs=[vmem] * 3,
        out_specs=vmem,
        cost_estimate=pl.CostEstimate(flops=0, bytes_accessed=2 << 20, transcendentals=0),
        compiler_params=pltpu.CompilerParams(vmem_limit_bytes=6 << 20),
        name="resid",
    )(total, other, data)


def fetches(pairs, sems, chunk):
    copies = []
    for j in range(pairs[0][1].shape[1] // chunk):
        cols = pl.ds(j * chunk, chunk)
        row = []
        for i, (source, target) in enumerate(pairs):
            copy = pltpu.make_async_copy(source.at[:, cols], target.at[:, cols], sems.at[i, j])
            copy.start()
            row.append(copy)
        copies.append(row)
    return copies


def corr_kernel(par, scale, lhs_first, lhs_second, own, near_source, out, acc, near, sems):
    even = par[0] == 0
    for j, copies in enumerate(fetches([(near_source, near)], sems, CORR_CHUNK)):
        for copy in copies:
            copy.wait()
        cols = pl.ds(j * CORR_CHUNK, CORR_CHUNK)
        near_cols = near[:, cols]
        rhs_first = jnp.where(even, own[:, cols], near_cols)
        near_scale = jnp.where(even, scale[:, cols], 1.0)
        rhs_second = (near_cols.astype(jnp.float32) * near_scale).astype(jnp.bfloat16)
        for pair, (lhs, rhs) in enumerate(((lhs_first, rhs_first), (lhs_second, rhs_second))):
            products = lax.dot_general(
                lhs[:, cols], rhs, (((1,), (1,)), ((), ())), preferred_element_type=jnp.float32
            )
            if j == 0:
                acc[pair] = products
            else:
                acc[pair] += products

    parts, _, _, rows, cols = out.shape
    half = parts * rows
    for pair in range(2):
        real = acc[pair, :half, :cols] + acc[pair, half:, cols:]
        imag = acc[pair, :half, cols:] - acc[pair, half:, :cols]
        out[:, pair, 0] = real.reshape(parts, rows, cols).astype(out.dtype)
        out[:, pair, 1] = imag.reshape(parts, rows, cols).astype(out.dtype)


def correlations(par, scale, lhs_first, lhs_second, own, near, parts):
    both, cols = own.shape
    half = both // 2
    vmem = pl.BlockSpec(memory_space=pltpu.VMEM)
    return pl.pallas_call(
        corr_kernel,
        out_shape=jax.ShapeDtypeStruct((parts, 2, 2, half // parts, half), WIRE),
        in_specs=[pl.BlockSpec(memory_space=pltpu.SMEM)] + [vmem] * 4 + [pl.BlockSpec(memory_space=pl.ANY)],
        out_specs=vmem,
        scratch_shapes=[
            pltpu.VMEM((2, both, both), jnp.float32),
            pltpu.VMEM((both, cols), jnp.bfloat16),
            pltpu.SemaphoreType.DMA((1, cols // CORR_CHUNK)),
        ],
        cost_estimate=pl.CostEstimate(flops=4 * both * both * cols, bytes_accessed=8 * both * cols, transcendentals=0),
        compiler_params=pltpu.CompilerParams(vmem_limit_bytes=24 << 20),
        name="corr",
    )(par, scale, lhs_first, lhs_second, own, near)


def assembled(gathered, pair, turned):
    real, imag = (gathered[:, pair, c].reshape(-1, gathered.shape[-1]) for c in range(2))
    if turned:
        real = real.astype(jnp.float32).T.astype(jnp.bfloat16)
        imag = (-imag.astype(jnp.float32)).T.astype(jnp.bfloat16)
    return real, imag


def place(mat, base, block):
    real, imag = block
    half = real.shape[0]
    mat[:half, base : base + half] = real
    mat[half:, base + half : base + 2 * half] = real
    mat[:half, base + half : base + 2 * half] = imag
    mat[half:, base : base + half] = -imag


def early_kernel(par, mine, own_source, mate_source, near_source, early, kernel_part, mat, own, blocks, out, sems, out_sems):
    both = own.shape[0]

    def run(even):
        parts = [(near_source, blocks.at[:both]), (mate_source, blocks.at[both:]), (own_source, own)]
        copies = fetches(parts, sems, CHUNK)
        place(mat, 0, assembled(mine, 1, False))
        place(mat, both, assembled(mine, 0, even))
        sends = []
        for j, row in enumerate(copies):
            for copy in row:
                copy.wait()
            cols = pl.ds(j * CHUNK, CHUNK)
            if even:
                fields = jnp.dot(mat[...], blocks[:, cols], preferred_element_type=jnp.float32)
            else:
                fields = jnp.dot(mat[:, :both], blocks[:both, cols], preferred_element_type=jnp.float32)
            out[j] = fields
            send = pltpu.make_async_copy(out.at[j], early.at[:, cols], out_sems.at[j])
            send.start()
            sends.append(send)
            share = own[:, cols].astype(jnp.float32) * fields
            if not even:
                other = jnp.dot(mat[:, both:], blocks[:both, cols], preferred_element_type=jnp.float32)
                share = share + blocks[both:, cols].astype(jnp.float32) * other
            kernel_part[:, cols] = jnp.sum(share, axis=0, keepdims=True)
        for send in sends:
            send.wait()

    @pl.when(par[0] == 0)
    def _():
        run(True)

    @pl.when(par[0] == 1)
    def _():
        run(False)


def turn_kernel(par, mate_resid, far_resid, mat):
    both = mat.shape[0]
    place(mat, 0, assembled(far_resid, 1, True))

    @pl.when(par[0] == 0)
    def _():
        place(mat, both, assembled(mate_resid, 0, False))

    @pl.when(par[0] == 1)
    def _():
        place(mat, both, assembled(far_resid, 0, True))
        place(mat, 2 * both, assembled(mate_resid, 0, False))


def late_kernel(inv_norm, par, scale, mat, early_source, far_real, far_imag, mate_source, mate_near_source, adjoint, blocks, early, out, sems, out_sems):
    both = early.shape[0]
    half = both // 2

    def run(even):
        depth = 2 * both if even else 3 * both
        parts = [
            (far_real, blocks.at[:half]),
            (far_imag, blocks.at[half:both]),
            (mate_near_source, blocks.at[both : 2 * both]),
            (early_source, early),
        ]
        if not even:
            parts.append((mate_source, blocks.at[2 * both :]))
        copies = fetches(parts, sems, CHUNK)
        sends = []
        for j, row in enumerate(copies):
            for copy in row:
                copy.wait()
            cols = pl.ds(j * CHUNK, CHUNK)
            fields = early[:, cols] + jnp.dot(
                mat[:, :depth], blocks[:depth, cols], preferred_element_type=jnp.float32
            )
            out[j] = (fields * (inv_norm * scale[:, cols])).reshape(out.shape[1:])
            send = pltpu.make_async_copy(out.at[j], adjoint.at[:, :, cols], out_sems.at[j])
            send.start()
            sends.append(send)
        for send in sends:
            send.wait()

    @pl.when(par[0] == 0)
    def _():
        run(True)

    @pl.when(par[0] == 1)
    def _():
        run(False)


def ring_kernel(place_of, rows, above, below, out, slots):
    count = slots.shape[0]
    position = 0
    for piece, offset in ((below, -3), (rows, -1), (above, 2)):
        for i in range(piece.shape[0]):
            slots[lax.rem(place_of[0] + (offset + i + count), count)] = piece[i]
            position += 1
    assert position == count
    total = slots[0]
    for i in range(1, count):
        total = total + slots[i]
    out[...] = total


def ring_sum(place_of, rows, above, below, count):
    vmem = pl.BlockSpec(memory_space=pltpu.VMEM)
    return pl.pallas_call(
        ring_kernel,
        out_shape=jax.ShapeDtypeStruct(rows.shape[1:], jnp.float32),
        in_specs=[pl.BlockSpec(memory_space=pltpu.SMEM)] + [vmem] * 3,
        out_specs=vmem,
        scratch_shapes=[pltpu.VMEM((count,) + rows.shape[1:], jnp.float32)],
        cost_estimate=pl.CostEstimate(flops=0, bytes_accessed=1 << 17, transcendentals=0),
        compiler_params=pltpu.CompilerParams(vmem_limit_bytes=1 << 20),
        name="ring_sum",
    )(place_of, rows, above, below)


def early_fields(par, mine, own, mate, near):
    both, cols = own.shape
    vmem = pl.BlockSpec(memory_space=pltpu.VMEM)
    anywhere = pl.BlockSpec(memory_space=pl.ANY)
    return pl.pallas_call(
        early_kernel,
        out_shape=(
            pltpu.HBM((both, cols), jnp.float32),
            jax.ShapeDtypeStruct((1, cols), jnp.float32),
        ),
        in_specs=[pl.BlockSpec(memory_space=pltpu.SMEM), vmem] + [anywhere] * 3,
        out_specs=(pl.BlockSpec(memory_space=pltpu.HBM), vmem),
        scratch_shapes=[pltpu.VMEM((both, 2 * both), jnp.bfloat16)]
        + [
            pltpu.VMEM((both, cols), jnp.bfloat16),
            pltpu.VMEM((2 * both, cols), jnp.bfloat16),
            pltpu.VMEM((cols // CHUNK, both, CHUNK), jnp.float32),
            pltpu.SemaphoreType.DMA((3, cols // CHUNK)),
            pltpu.SemaphoreType.DMA((cols // CHUNK,)),
        ],
        cost_estimate=pl.CostEstimate(flops=4 * both * both * cols, bytes_accessed=10 * both * cols, transcendentals=0),
        compiler_params=pltpu.CompilerParams(vmem_limit_bytes=20 << 20),
        name="early",
    )(par, mine, own, mate, near)


def turned(par, mate_resid, far_resid, both):
    vmem = pl.BlockSpec(memory_space=pltpu.VMEM)
    return pl.pallas_call(
        turn_kernel,
        out_shape=jax.ShapeDtypeStruct((both, 3 * both), jnp.bfloat16),
        in_specs=[pl.BlockSpec(memory_space=pltpu.SMEM), vmem, vmem],
        out_specs=vmem,
        cost_estimate=pl.CostEstimate(flops=0, bytes_accessed=2 << 20, transcendentals=0),
        compiler_params=pltpu.CompilerParams(vmem_limit_bytes=8 << 20),
        name="turned",
    )(par, mate_resid, far_resid)


def late_fields(par, scale, mat, far, early, mate, mate_near, inv_norm):
    both, cols = early.shape
    half = both // 2
    vmem = pl.BlockSpec(memory_space=pltpu.VMEM)
    hbm = pl.BlockSpec(memory_space=pltpu.HBM)

    def body(*refs):
        late_kernel(inv_norm, *refs)

    return pl.pallas_call(
        body,
        out_shape=jax.ShapeDtypeStruct((2, half, cols), jnp.float32),
        in_specs=[pl.BlockSpec(memory_space=pltpu.SMEM)] + [vmem] * 2 + [hbm] * 5,
        out_specs=hbm,
        scratch_shapes=[
            pltpu.VMEM((3 * both, cols), jnp.bfloat16),
            pltpu.VMEM((both, cols), jnp.float32),
            pltpu.VMEM((cols // CHUNK, 2, half, CHUNK), jnp.float32),
            pltpu.SemaphoreType.DMA((5, cols // CHUNK)),
            pltpu.SemaphoreType.DMA((cols // CHUNK,)),
        ],
        cost_estimate=pl.CostEstimate(flops=4 * both * both * cols, bytes_accessed=12 * both * cols, transcendentals=0),
        compiler_params=pltpu.CompilerParams(vmem_limit_bytes=48 << 20),
        name="late",
    )(par, scale, mat, early, *far, mate, mate_near)


def shards(green, source_weight, observed, amp_weight, pair_used):
    row_count, col_count = green.shape[1:]
    block_count = lax.axis_size("cable")
    parts = lax.axis_size("grid")
    inv_norm = 1.0 / math.sqrt(col_count * parts)
    kernel_scale = inv_norm / (2.0 * math.sqrt(2.0 * block_count))
    parity = lax.axis_index("cable") % 2
    even = parity == 0
    par = parity.reshape(1)
    scale = source_weight[None, :]
    own = green.reshape(2 * row_count, col_count)
    pieces_count = parts // 2
    along_x = [list(range(i, parts, 2)) for i in range(2)]

    near = permuted(own, "cable", near_chip)
    mate = permuted(own, "cable", partner)

    slice_rows = row_count // pieces_count
    first = lax.axis_index("grid") // 2 * slice_rows
    packed = prepared(par, pair_used, first.reshape(1), observed, amp_weight, slice_rows)
    data_first = permuted(packed[0], "cable", partner)
    data_second = permuted(packed[1], "cable", near_chip)
    data = jnp.stack([data_first, jnp.where(even, data_second, packed[1])])

    lhs_first = (mate.astype(jnp.float32) * scale).astype(jnp.bfloat16)
    lhs_second = (own.astype(jnp.float32) * jnp.where(even, 1.0, scale)).astype(jnp.bfloat16)
    cuts = (green[0], green[1])
    near, lhs_first, lhs_second, cuts = lax.optimization_barrier((near, lhs_first, lhs_second, cuts))

    partials = correlations(par, scale, lhs_first, lhs_second, own, near, pieces_count)
    far = []
    for component in range(2):
        far.append(permuted(cuts[component], "cable", far_chip))
    mate_near = permuted(near, "cable", partner)
    pieces = lax.all_to_all(partials, "grid", 0, 0, tiled=True, axis_index_groups=along_x)
    total, wire = summed(pieces)
    other = permuted(wire, "grid", partner)
    resid = residuals(total, other, data, pieces_count, inv_norm)
    mine = lax.all_to_all(resid, "grid", 0, 0, tiled=True, axis_index_groups=along_x)
    mate_resid = permuted(mine[:, :1], "cable", partner)
    far_resid = permuted(mine, "cable", far_chip)
    early, kernel_part = early_fields(par, mine, own, mate, near)
    kernel = kernel_part[0] * kernel_scale
    mat = turned(par, mate_resid, far_resid, 2 * row_count)
    adjoint = late_fields(par, scale, mat, far, early, mate, mate_near, inv_norm)
    distance = block_count // 2
    swapped = [permuted(kernel, "cable", lambda i: i ^ d) for d in (1, distance, distance + 1)]
    kernel = (kernel + swapped[0]) + (swapped[1] + swapped[2])

    def along_z(hops):
        return lambda i: i // distance * distance + (i + 2 * hops) % distance

    kernel = kernel.reshape(1, 16, -1)
    neighbours = [permuted(kernel, "cable", along_z(hops)) for hops in (-1, 1)]
    rows = jnp.concatenate([neighbours[0], kernel, neighbours[1]], axis=0)
    above = permuted(rows, "cable", along_z(3))
    below = permuted(rows[1:], "cable", along_z(-3))
    place_of = lax.axis_index("cable") % distance // 2
    kernel = ring_sum(place_of.reshape(1), rows, above, below, distance // 2).reshape(col_count)
    return (adjoint, kernel)


def solution(mesh):
    in_specs = (
        P(None, "cable", "grid"),
        P("grid"),
        P(None, None, "cable", None),
        P(None, "cable", None),
        P("cable", None),
    )
    out_specs = (P(None, "cable", "grid"), P("grid"))

    return jax.shard_map(shards, mesh=mesh, in_specs=in_specs, out_specs=out_specs, check_vma=False)
```
